128 devices in a mesh: days: 8 (over x, core), fac: 16 (over y, z).
Axes of the slice: x: 4, y: 4, z: 4, core: 2. Of those that a mesh axis runs over, the one named last changes fastest.
Arguments:
- history: bfloat16 [4096, 16384], P('days', 'fac'), may hold values from -1.796875 to 1.796875
- block_starts: int32 [2048, 4], replicated, may hold values from 0 to 4092
- block_lengths: int32 [2048, 4], replicated, may hold values from 1 to 4, 10 in all within a row
- vol_scale: float32 [16384], P('fac'), may hold values from 0.5 to 2
- exposure: bfloat16 [8192, 16384], P('days', 'fac'), may hold values from -0.046875 to 0.046875
- realized: bfloat16 [16384], P('fac'), may hold values from -6 to 6
Outputs:
- path_loss: bfloat16 [8192, 2048], P(('days', 'fac'))
- margin: float32 [8192], P(('days', 'fac'))
- shortfall: float32 [8192], P(('days', 'fac'))
The draws below stay inside these ranges and needn't reach their ends.
Inputs may be any that keep to these rules, and one draw needn't show every extreme that they name: `block_starts`: every block lies inside the history: a start is at most 4092. `block_lengths`: the 4 lengths of a path sum to 10.
All inputs are finite; a program needn't handle non-finite values.
Results may differ from the reference program's by a relative error of at most 0.019.
Values may be sent and summed in bfloat16 or wider, within the bound.
A program may use at most 64 MiB of HBM per device.

```python
import math
import jax
import jax.numpy as jnp
import numpy as np
from jax import lax

FACTORS = 16384
ACCOUNTS = 8192
PATHS = 2048
HORIZON = 10
NBLK = 4
MOSTLEN = 4
DAYS = 4096
N_FAC = 16


def touch_ends(array, key, smallest, largest):
    spot = [jax.random.randint(jax.random.fold_in(key, axis), (), 0, length) for axis, length in enumerate(array.shape)]
    main_axis = array.shape.index(max(array.shape))
    beside = spot[:main_axis] + [(spot[main_axis] + 1) % array.shape[main_axis]] + spot[main_axis + 1:]
    return array.at[tuple(spot)].set(smallest).at[tuple(beside)].set(largest)


def block_levels(own_key, dims, pieces, low, high):
    def one(position, blocks):
        heights = jax.random.uniform(jax.random.fold_in(jax.random.fold_in(own_key, 6), position), (blocks,), jnp.float32, low / len(pieces), high / len(pieces))
        return jnp.repeat(jnp.exp(heights), dims[position] // blocks).reshape((-1,) + (1,) * (len(dims) - position - 1))

    factor_of = one(*pieces[0])
    for cut in pieces[1:]:
        factor_of = factor_of * one(*cut)
    return factor_of


def rank_bounds(number_of, lean):
    loads = [(1 << 20) // math.isqrt(grade ** lean) + 1 for grade in range(1, number_of + 1)]
    deviation = 1 + sum(loads) // (1 << 30)
    return np.cumsum(np.array([max(1, weight // deviation) for weight in loads]))


def ranked(key, extent, amount, slope):
    table = rank_bounds(amount, slope)
    ticket = jax.random.randint(jax.random.fold_in(key, 1), extent, 0, int(table[amount - 1]))
    rank = jnp.searchsorted(jnp.asarray(table, jnp.int32), ticket, side="right")
    return jax.random.permutation(jax.random.fold_in(key, 2), amount)[rank].astype(jnp.int32)


def split_up(amount, total, limit, lean):
    portions = [(1 << 20) // math.isqrt(grade ** lean) + 1 for grade in range(2, amount + 1)]
    surplus, given = total - limit - (amount - 1), [1] * (amount - 1)
    while surplus > 0:
        candidates = [i for i in range(amount - 1) if given[i] < limit]
        mass, remaining = sum([portions[i] for i in candidates]), surplus
        for i in candidates:
            addition = min(limit - given[i], max(1, remaining * portions[i] // mass), surplus)
            given[i] = given[i] + addition
            surplus = surplus - addition
    return np.array([limit] + given)


def uneven_parts(rng, number_of, total, bound, slope):
    if number_of == 2:
        one = jax.random.randint(rng, (), max(1, total - bound), min(bound, total - 1) + 1)
        return jnp.stack([one, total - one])
    sizes = jnp.asarray(split_up(number_of, total, bound, slope), jnp.int32)
    pairs = (number_of - 1) // 2
    donor, receiver = sizes[1:1 + 2 * pairs:2], sizes[2:2 + 2 * pairs:2]
    room = jnp.minimum(donor - 1, bound - receiver)
    passed = jax.random.randint(jax.random.fold_in(rng, 1), (pairs,), 0, 1 << 20) % (room + 1)
    sizes = sizes.at[1:1 + 2 * pairs:2].set(donor - passed).at[2:2 + 2 * pairs:2].set(receiver + passed)
    return sizes[jax.random.permutation(jax.random.fold_in(rng, 2), number_of)]


def scatter_about(stream_key, dims, deviation, limit, shards=(), kind=jnp.bfloat16):
    gain = block_levels(stream_key, dims, shards, -0.22, 0.18) if shards else 1.0
    drawn = jax.random.normal(stream_key, dims, jnp.float32) * deviation * gain
    return jnp.minimum(jnp.maximum(drawn, -limit), limit).astype(kind)


def setup_inputs(seed: int = 0) -> dict:
    seeds = jax.random.split(jax.random.key(seed), 7)
    return {
        "history": scatter_about(seeds[0], (DAYS, FACTORS), 0.3, 1.796875, ((0, 8), (1, 16))),
        "block_starts": touch_ends(ranked(seeds[1], (PATHS, NBLK), DAYS - MOSTLEN + 1, 2), jax.random.fold_in(seeds[1], 3), 0, DAYS - MOSTLEN).astype(jnp.int32),
        "block_lengths": jax.vmap(lambda own: uneven_parts(own, NBLK, HORIZON, MOSTLEN, 2))(jax.random.split(seeds[2], PATHS)).reshape((PATHS, NBLK)).astype(jnp.int32),
        "vol_scale": jnp.clip(jnp.exp(math.log(2.0) - 1.3862944 * jax.random.uniform(seeds[3], (FACTORS,), jnp.float32) ** block_levels(seeds[3], (FACTORS,), ((0, 16),), -0.2, 0.2)), 0.5, 2.0),
        "exposure": scatter_about(seeds[4], (ACCOUNTS, FACTORS), FACTORS ** -0.5, 0.046875, ((0, 8), (1, 16))),
        "realized": scatter_about(seeds[5], (FACTORS,), 1.0, 6.0, ((0, 16),)),
    }


def reference(history, block_starts, block_lengths, vol_scale, exposure, realized):
    path_sum = jnp.zeros((PATHS, FACTORS), jnp.float32)
    for block in range(NBLK):
        for offset in range(MOSTLEN):
            rows = (block_starts[:, block] + offset).astype(jnp.int32)
            inside = (offset < block_lengths[:, block]).astype(jnp.float32)
            picked = jnp.take(history, rows, axis=0).astype(jnp.float32)
            path_sum = path_sum + inside[:, None] * picked
    shock = (path_sum * vol_scale[None, :]).astype(jnp.bfloat16)
    width = FACTORS // N_FAC

    def add_group(carry, group):
        loss_total, real_total = carry
        first = (group * width).astype(jnp.int32)
        expo = lax.dynamic_slice_in_dim(exposure, first, width, 1)
        shock_part = lax.dynamic_slice_in_dim(shock, first, width, 1)
        real_piece = lax.dynamic_slice_in_dim(realized, first, width, 0)
        loss_part = -lax.dot_general(expo, shock_part, (((1,), (1,)), ((), ())), preferred_element_type=jnp.float32)
        real_part = -jnp.dot(expo, real_piece, preferred_element_type=jnp.float32)
        loss_part = lax.optimization_barrier(loss_part.astype(jnp.bfloat16))
        real_part = lax.optimization_barrier(real_part.astype(jnp.bfloat16))
        return (loss_total + loss_part.astype(jnp.float32), real_total + real_part.astype(jnp.float32)), None

    start = (jnp.zeros((ACCOUNTS, PATHS), jnp.float32), jnp.zeros((ACCOUNTS,), jnp.float32))
    (loss, realized_loss), unused = lax.scan(add_group, start, jnp.arange(N_FAC, dtype=jnp.int32))
    margin = jnp.log(jnp.mean(jnp.exp(loss), axis=1))
    return loss.astype(jnp.bfloat16), margin, realized_loss - margin
```

```python
import functools

import jax
import jax.numpy as jnp
from jax import lax
from jax.experimental import pallas as pl
from jax.experimental.pallas import tpu as pltpu
from jax.sharding import PartitionSpec as P

CHUNKS = 8
STEPS = 4
ORDERS = (
    ("zu", "yu", "zv", "yv"),
    ("zv", "yv", "zu", "yu"),
    ("yu", "zu", "yv", "zv"),
    ("yv", "zv", "yu", "zu"),
)


def bits(place):
    return (place % 2 + place // 2) % 2, place // 2


def slot_of(order, fac):
    yu, yv = bits(fac // 4)
    zu, zv = bits(fac % 4)
    value = {"yu": yu, "yv": yv, "zu": zu, "zv": zv}
    slot = 0
    for name in order:
        slot = slot * 2 + value[name]
    return slot


def remote(src, dst, send, recv, device):
    return pltpu.make_async_remote_copy(
        src_ref=src,
        dst_ref=dst,
        send_sem=send,
        recv_sem=recv,
        device_id=device,
        device_id_type=pl.DeviceIdType.MESH,
    )


def kernel(
    hist, starts, lens, vol, expo, real,
    out, margin, shortfall,
    days, book, counts, part, part_in, pair, pair_in, shock,
    loss0, loss1, loss2, loss3, in0, in1, in2, in3, sums, owed,
    here, days_send, days_recv, x_send, x_recv, sib_send, sib_recv, f_send, f_recv,
):
    own_days, width = hist.shape
    paths = starts.shape[1]
    d = lax.axis_index("days")
    f = lax.axis_index("fac")
    x, c = d // 2, d % 2
    y, z = f // 4, f % 4
    u, v = bits(x)
    yu, yv = bits(y)
    zu, zv = bits(z)
    sibling = {"days": x * 2 + 1 - c}
    over_u = {"days": (x + 1 - 2 * (x % 2)) * 2 + c}
    over_v = {"days": (3 - x) * 2 + c}
    place = {"yu": yu, "yv": yv, "zu": zu, "zv": zv}
    partner = {
        "zu": {"fac": y * 4 + z + 1 - 2 * (z % 2)},
        "zv": {"fac": y * 4 + 3 - z},
        "yu": {"fac": (y + 1 - 2 * (y % 2)) * 4 + z},
        "yv": {"fac": (3 - y) * 4 + z},
    }
    first, second = (u, v), (v, u)
    over_first, over_second = (over_u, over_v), (over_v, over_u)
    losses, arrivals = (loss0, loss1, loss2, loss3), (in0, in1, in2, in3)

    load_book = pltpu.make_async_copy(expo, book, here.at[0])
    load_days = pltpu.make_async_copy(hist, days.at[c], here.at[1])
    load_days.start()
    load_book.start()
    barrier = pltpu.get_barrier_semaphore()
    everyone = (sibling, over_u, over_v, *partner.values())
    for device in everyone:
        pl.semaphore_signal(barrier, inc=1, device_id=device, device_id_type=pl.DeviceIdType.MESH)
    pl.semaphore_wait(barrier, len(everyone))

    share_days = remote(hist, days.at[c], days_send, days_recv, sibling)
    share_days.start()

    shock[0] = jnp.zeros(shock.shape[1:], shock.dtype)
    rows = lax.broadcasted_iota(jnp.int32, (16, width), 0)
    moved = jnp.broadcast_to(-real[...].astype(jnp.float32), (16, width))
    shock[0, 0, 0, 0, 0] = jnp.where(rows == 0, moved, 0.0).astype(shock.dtype)
    sums[...] = jnp.zeros_like(sums)

    half = paths // CHUNKS // 2
    chip_days = 2 * own_days

    def count_days(q, carry):
        at = pl.multiple_of((q * 2 + c) * half, half)
        low = starts[:, pl.ds(at, half)]
        both = jnp.concatenate([low, low + lens[:, pl.ds(at, half)]], axis=0).astype(jnp.float32)
        table = jnp.concatenate([both] * (half // 8), axis=0).T
        day = (lax.broadcasted_iota(jnp.int32, (16, chip_days), 1) + x * chip_days).astype(jnp.float32)
        for group in range(half // 16):
            piece = table[group * 16 : group * 16 + 16]
            total = jnp.zeros((16, chip_days), jnp.float32)
            for block in range(4):
                inside = (day >= piece[:, block : block + 1]) & (day < piece[:, block + 4 : block + 5])
                total = total + jnp.where(inside, 1.0, 0.0)
            counts[q, group * 16 : group * 16 + 16, :] = total.astype(counts.dtype)
        return carry

    lax.fori_loop(0, CHUNKS, count_days, 0)
    load_days.wait()
    share_days.wait()
    load_book.wait()

    def scatter_one(q, s):
        return remote(part.at[q, s, 1 - first[s]], part_in.at[q, s], x_send.at[0, s], x_recv.at[0, s, q], over_first[s])

    def scatter_two(q, s):
        return remote(pair.at[q, s, 1 - second[s]], pair_in.at[q, s], x_send.at[1, s], x_recv.at[1, s, q], over_second[s])

    def gather_one(q, s, block):
        rows = shock.at[q + 1, c, s, first[s], block]
        return remote(rows, rows, x_send.at[2, s], x_recv.at[2, s, q], over_second[s])

    def gather_two(q, s, block):
        rows = shock.at[q + 1, c, s, block]
        return remote(rows, rows, x_send.at[3, s], x_recv.at[3, s, q], over_first[s])

    def give_sibling(q, core):
        rows = shock.at[q + 1, core]
        return remote(rows, rows, sib_send, sib_recv.at[q], sibling)

    def pass_losses(step, r, k):
        name = ORDERS[k][step]
        return remote(
            losses[step].at[r, k, 1 - place[name]], arrivals[step].at[r, k],
            f_send.at[step, k], f_recv.at[step, k, r], partner[name],
        )

    def launch(copy, turn):
        @pl.when(turn > 0)
        def _():
            copy.wait_send()
        copy.start()

    def stage(turn, count, body):
        @pl.when((turn >= 0) & (turn < count))
        def _():
            body(turn)

    def sum_days(q):
        whole = days[...].reshape(chip_days, width)
        total = jnp.dot(counts[q], whole, preferred_element_type=jnp.float32).astype(part.dtype)
        part[q] = total.reshape(part.shape[1:])
        for s in range(2):
            launch(scatter_one(q, s), q)

    def sum_pairs(q):
        for s in range(2):
            scatter_one(q, s).wait_recv()
            total = part[q, s, first[s]].astype(jnp.float32) + part_in[q, s].astype(jnp.float32)
            pair[q, s] = total.astype(pair.dtype).reshape(pair.shape[2:])
            launch(scatter_two(q, s), q)

    def sum_chips(q):
        for s in range(2):
            scatter_two(q, s).wait_recv()
            total = pair[q, s, second[s]].astype(jnp.float32) + pair_in[q, s].astype(jnp.float32)
            shock[q + 1, c, s, first[s], second[s]] = (total * -vol[...]).astype(shock.dtype)
            launch(gather_one(q, s, second[s]), q)

    def spread(q):
        for s in range(2):
            gather_one(q, s, 1 - second[s]).wait_recv()
            launch(gather_two(q, s, first[s]), q)

    def cross(q):
        for s in range(2):
            gather_two(q, s, 1 - first[s]).wait_recv()
        launch(give_sibling(q, c), q)

    def revalue(r):
        @pl.when(r > 0)
        def _():
            give_sibling(r - 1, 1 - c).wait_recv()
        moves = shock[r].reshape(2 * half, width)
        value = lax.dot_general(
            book[...], moves, (((1,), (1,)), ((), ())), preferred_element_type=jnp.float32
        ).astype(loss0.dtype)
        span = loss0.shape[3] // 8
        for k in range(4):
            lane, row = k // 2 * 128, k % 2 * span
            for owner in range(16):
                slot = slot_of(ORDERS[k], owner)
                at = slot % 8 * span
                loss0[r, k, slot // 8, at : at + span, :] = value[
                    owner * 2 * span + row : owner * 2 * span + row + span, lane : lane + 128
                ]
            launch(pass_losses(0, r, k), r)

    def fold(step, r):
        for k in range(4):
            pass_losses(step - 1, r, k).wait_recv()
            kept = losses[step - 1][r, k, place[ORDERS[k][step - 1]]]
            total = kept.astype(jnp.float32) + arrivals[step - 1][r, k].astype(jnp.float32)
            losses[step][r, k] = total.astype(loss0.dtype).reshape(losses[step].shape[2:])
            launch(pass_losses(step, r, k), r)

    def finish(r):
        span = in3.shape[2]
        for k in range(4):
            pass_losses(3, r, k).wait_recv()
            kept = loss3[r, k, place[ORDERS[k][3]]]
            loss = kept.astype(jnp.float32) + in3[r, k].astype(jnp.float32)
            lane, row = k // 2 * 128, k % 2 * span

            @pl.when(r > 0)
            def _():
                at = pl.multiple_of((r - 1) * 2 * half + lane, 128)
                out[row : row + span, pl.ds(at, 128)] = loss.astype(out.dtype)
                sums[row : row + span, :] = sums[row : row + span, :] + jnp.exp(loss)

            if lane == 0:

                @pl.when(r == 0)
                def _():
                    owed[row : row + span, :] = loss

    def turn(t, carry):
        stage(t - 1, CHUNKS, sum_pairs)
        stage(t - 2, CHUNKS, sum_chips)
        stage(t - 3, CHUNKS, spread)
        stage(t - 4, CHUNKS, cross)
        stage(t, CHUNKS, sum_days)
        stage(t - 4, CHUNKS + 1, revalue)
        for step in range(1, 4):
            stage(t - 4 - step, CHUNKS + 1, functools.partial(fold, step))
        stage(t - 8, CHUNKS + 1, finish)
        return carry

    lax.fori_loop(0, CHUNKS + 9, turn, 0)

    last = CHUNKS - 1
    for s in range(2):
        scatter_one(last, s).wait_send()
        scatter_two(last, s).wait_send()
        gather_one(last, s, second[s]).wait_send()
        gather_two(last, s, first[s]).wait_send()
    give_sibling(last, c).wait_send()
    for k in range(4):
        for step in range(4):
            pass_losses(step, CHUNKS, k).wait_send()

    count = out.shape[0]
    level = jnp.log(jnp.sum(sums[...], axis=1, keepdims=True) * (1.0 / paths))
    diagonal = lax.broadcasted_iota(jnp.int32, (count, count), 0) == lax.broadcasted_iota(
        jnp.int32, (count, count), 1
    )
    margin[...] = jnp.sum(jnp.where(diagonal, level, 0.0), axis=0, keepdims=True)
    over = owed[:, 0:1] - level
    shortfall[...] = jnp.sum(jnp.where(diagonal, over, 0.0), axis=0, keepdims=True)


def local(history, block_starts, block_lengths, vol_scale, exposure, realized):
    own_days, width = history.shape
    paths = block_starts.shape[0]
    accounts = exposure.shape[0]
    mine = accounts // 16
    q, r = CHUNKS, CHUNKS + 1
    half = paths // q // 2
    block = half // 8
    whole = functools.partial(pl.BlockSpec, memory_space=pltpu.VMEM)
    raw = pl.BlockSpec(memory_space=pl.ANY)
    bf16, f32 = jnp.bfloat16, jnp.float32
    quarter = mine // 2
    dma = pltpu.SemaphoreType.DMA
    out, margin, shortfall = pl.pallas_call(
        kernel,
        out_shape=(
            jax.ShapeDtypeStruct((mine, paths), bf16),
            jax.ShapeDtypeStruct((1, mine), f32),
            jax.ShapeDtypeStruct((1, mine), f32),
        ),
        in_specs=[raw, whole(), whole(), whole(), raw, whole()],
        out_specs=(whole(), whole(), whole()),
        scratch_shapes=[
            pltpu.VMEM((2, own_days, width), bf16),
            pltpu.VMEM((accounts, width), bf16),
            pltpu.VMEM((q, half, 2 * own_days), bf16),
            pltpu.VMEM((q, 2, 2, 2 * block, width), bf16),
            pltpu.VMEM((q, 2, 2 * block, width), bf16),
            pltpu.VMEM((q, 2, 2, block, width), bf16),
            pltpu.VMEM((q, 2, block, width), bf16),
            pltpu.VMEM((r, 2, 2, 2, 2, block, width), bf16),
            *[pltpu.VMEM((r, 4, 2, (8 >> step) * quarter, 128), bf16) for step in range(4)],
            *[pltpu.VMEM((r, 4, (8 >> step) * quarter, 128), bf16) for step in range(4)],
            pltpu.VMEM((mine, 128), f32),
            pltpu.VMEM((mine, 128), f32),
            dma((2,)),
            dma,
            dma,
            dma((4, 2)),
            dma((4, 2, q)),
            dma,
            dma((q,)),
            dma((4, 4)),
            dma((4, 4, r)),
        ],
        compiler_params=pltpu.CompilerParams(
            collective_id=0, has_side_effects=True, vmem_limit_bytes=56 << 20
        ),
        name="backtest",
    )(
        history,
        block_starts.T,
        block_lengths.T,
        vol_scale.reshape(1, width),
        exposure,
        realized.reshape(1, width),
    )
    return out, margin.reshape(mine), shortfall.reshape(mine)


def solution(mesh):
    in_specs = (P("days", "fac"), P(), P(), P("fac"), P("days", "fac"), P("fac"))
    out_specs = (P(("days", "fac"), None), P(("days", "fac")), P(("days", "fac")))
    return jax.shard_map(local, mesh=mesh, in_specs=in_specs, out_specs=out_specs, check_vma=False)
```

```python
import functools

import jax
import jax.numpy as jnp
from jax import lax
from jax.experimental import pallas as pl
from jax.experimental.pallas import tpu as pltpu
from jax.sharding import PartitionSpec as P

CHUNKS = 8
PAIRS, CHIPS, SPREAD, CROSS, REVALUE, FOLD, FINISH = 2, 3, 4, 5, 5, 6, 7


def bits(place):
    return (place % 2 + place // 2) % 2, place // 2


def remote(src, dst, send, recv, device):
    return pltpu.make_async_remote_copy(
        src_ref=src,
        dst_ref=dst,
        send_sem=send,
        recv_sem=recv,
        device_id=device,
        device_id_type=pl.DeviceIdType.MESH,
    )


def kernel(
    hist, starts, lens, vol, expo, real,
    out, margin, shortfall,
    days, book, counts, part, part_in, pair, pair_in, shock,
    loss, loss_in, row, row_in, sums, owed,
    here, days_send, days_recv, x_send, x_recv, sib_send, sib_recv, f_send, f_recv,
):
    own_days, width = hist.shape
    paths = starts.shape[1]
    d = lax.axis_index("days")
    f = lax.axis_index("fac")
    x, c = d // 2, d % 2
    y, z = f // 4, f % 4
    u, v = bits(x)
    sibling = {"days": x * 2 + 1 - c}
    over_u = {"days": (x + 1 - 2 * (x % 2)) * 2 + c}
    over_v = {"days": (3 - x) * 2 + c}
    over_y = [{"fac": (y + j) % 4 * 4 + z} for j in range(1, 4)]
    over_z = [{"fac": y * 4 + (z + j) % 4} for j in range(1, 4)]
    first, second = (u, v), (v, u)
    over_first, over_second = (over_u, over_v), (over_v, over_u)
    place = ((z, y), (y, z))
    over_place = ((over_z, over_y), (over_y, over_z))

    load_book = pltpu.make_async_copy(expo, book, here.at[0])
    load_days = pltpu.make_async_copy(hist, days.at[c], here.at[1])
    load_days.start()
    load_book.start()
    barrier = pltpu.get_barrier_semaphore()
    everyone = (sibling, over_u, over_v, *over_y, *over_z)
    for device in everyone:
        pl.semaphore_signal(barrier, inc=1, device_id=device, device_id_type=pl.DeviceIdType.MESH)
    pl.semaphore_wait(barrier, len(everyone))

    share_days = remote(hist, days.at[c], days_send, days_recv, sibling)
    share_days.start()

    shock[0] = jnp.zeros(shock.shape[1:], shock.dtype)
    lead = shock.shape[5]
    rows = lax.broadcasted_iota(jnp.int32, (lead, width), 0)
    moved = jnp.broadcast_to(-real[...].astype(jnp.float32).reshape(1, width), (lead, width))
    shock[0, 0, 0, 0, 0] = jnp.where(rows == 0, moved, 0.0).astype(shock.dtype)
    sums[...] = jnp.zeros_like(sums)

    half = paths // CHUNKS // 2
    chip_days = 2 * own_days
    mine = out.shape[0]

    def count_days(q):
        at = pl.multiple_of((q * 2 + c) * half, half)
        low = starts[:, pl.ds(at, half)]
        both = jnp.concatenate([low, low + lens[:, pl.ds(at, half)]], axis=0).astype(jnp.float32)
        table = jnp.concatenate([both] * (half // 8), axis=0).T
        day = (lax.broadcasted_iota(jnp.int32, (16, chip_days), 1) + x * chip_days).astype(jnp.float32)
        for group in range(half // 16):
            piece = table[group * 16 : group * 16 + 16]
            total = jnp.zeros((16, chip_days), jnp.float32)
            for block in range(4):
                inside = (day >= piece[:, block : block + 1]) & (day < piece[:, block + 4 : block + 5])
                total = total + jnp.where(inside, 1.0, 0.0)
            counts[q, group * 16 : group * 16 + 16, :] = total.astype(counts.dtype)

    count_days(0)
    load_days.wait()
    share_days.wait()

    def scatter_one(q, s):
        return remote(part.at[q, s, 1 - first[s]], part_in.at[q, s], x_send.at[0, s, q], x_recv.at[0, s, q], over_first[s])

    def scatter_two(q, s):
        return remote(pair.at[q, s, 1 - second[s]], pair_in.at[q, s], x_send.at[1, s, q], x_recv.at[1, s, q], over_second[s])

    def gather_one(q, s, block):
        rows = shock.at[q + 1, c, s, first[s], block]
        return remote(rows, rows, x_send.at[2, s, q], x_recv.at[2, s, q], over_second[s])

    def gather_two(q, s, block):
        rows = shock.at[q + 1, c, s, block]
        return remote(rows, rows, x_send.at[3, s, q], x_recv.at[3, s, q], over_first[s])

    def give_sibling(q, core):
        rows = shock.at[q + 1, core]
        return remote(rows, rows, sib_send.at[q], sib_recv.at[q], sibling)

    def pass_loss(r, h, j):
        return remote(
            loss.at[r, h, (place[h][0] + j) % 4], loss_in.at[r, h, j - 1],
            f_send.at[0, h, j - 1, r], f_recv.at[0, h, j - 1, r], over_place[h][0][j - 1],
        )

    def pass_row(r, h, j):
        return remote(
            row.at[r, h, (place[h][1] + j) % 4], row_in.at[r, h, j - 1],
            f_send.at[1, h, j - 1, r], f_recv.at[1, h, j - 1, r], over_place[h][1][j - 1],
        )

    def stage(turn, count, body):
        @pl.when((turn >= 0) & (turn < count))
        def _():
            body(turn)

    def sum_days(q):
        whole = days[...].reshape(chip_days, width)
        total = jnp.dot(counts[q], whole, preferred_element_type=jnp.float32).astype(part.dtype)
        part[q] = total.reshape(part.shape[1:])
        for s in range(2):
            scatter_one(q, s).start()

    def sum_pairs(q):
        for s in range(2):
            scatter_one(q, s).wait_recv()
            total = part[q, s, first[s]].astype(jnp.float32) + part_in[q, s].astype(jnp.float32)
            pair[q, s] = total.astype(pair.dtype).reshape(pair.shape[2:])
            scatter_two(q, s).start()

    def sum_chips(q):
        for s in range(2):
            scatter_two(q, s).wait_recv()
            total = pair[q, s, second[s]].astype(jnp.float32) + pair_in[q, s].astype(jnp.float32)
            shock[q + 1, c, s, first[s], second[s]] = (total * -vol[...]).astype(shock.dtype)
            gather_one(q, s, second[s]).start()

    def spread(q):
        for s in range(2):
            gather_one(q, s, 1 - second[s]).wait_recv()
            gather_two(q, s, first[s]).start()

    def cross(q):
        for s in range(2):
            gather_two(q, s, 1 - first[s]).wait_recv()
        give_sibling(q, c).start()

    def revalue(r):
        @pl.when(r == 0)
        def _():
            load_book.wait()

        @pl.when(r > 0)
        def _():
            give_sibling(r - 1, 1 - c).wait_recv()

        moves = shock[r].reshape(2 * half, width)
        value = lax.dot_general(
            book[...], moves, (((1,), (1,)), ((), ())), preferred_element_type=jnp.float32
        ).astype(loss.dtype)
        for h in range(2):
            for owner in range(16):
                at = (owner // 4, owner % 4) if h else (owner % 4, owner // 4)
                loss[r, h, at[0], at[1]] = value[owner * mine : owner * mine + mine, h * half : h * half + half]
            for j in range(1, 4):
                pass_loss(r, h, j).start()

    def fold(r):
        for h in range(2):
            total = loss[r, h, place[h][0]].astype(jnp.float32)
            for j in range(1, 4):
                pass_loss(r, h, j).wait_recv()
                total = total + loss_in[r, h, j - 1].astype(jnp.float32)
            row[r, h] = total.astype(row.dtype)
            for j in range(1, 4):
                pass_row(r, h, j).start()

    def finish(r):
        for h in range(2):
            total = row[r, h, place[h][1]].astype(jnp.float32)
            for j in range(1, 4):
                pass_row(r, h, j).wait_recv()
                total = total + row_in[r, h, j - 1].astype(jnp.float32)

            @pl.when(r > 0)
            def _():
                at = pl.multiple_of(((r - 1) * 2 + h) * half, half)
                out[:, pl.ds(at, half)] = total.astype(out.dtype)
                sums[...] = sums[...] + jnp.exp(total)

            if h == 0:

                @pl.when(r == 0)
                def _():
                    owed[...] = total

    def turn(t, carry):
        stage(t - PAIRS, CHUNKS, sum_pairs)
        stage(t - CHIPS, CHUNKS, sum_chips)
        stage(t - SPREAD, CHUNKS, spread)
        stage(t - CROSS, CHUNKS, cross)
        stage(t, CHUNKS, sum_days)
        stage(t + 1, CHUNKS, count_days)
        stage(t - REVALUE, CHUNKS + 1, revalue)
        stage(t - FOLD, CHUNKS + 1, fold)
        stage(t - FINISH, CHUNKS + 1, finish)
        return carry

    lax.fori_loop(0, CHUNKS + 1 + FINISH, turn, 0)

    level = jnp.log(jnp.sum(sums[...], axis=1, keepdims=True) * (1.0 / paths))
    diagonal = lax.broadcasted_iota(jnp.int32, (mine, mine), 0) == lax.broadcasted_iota(
        jnp.int32, (mine, mine), 1
    )
    margin[...] = jnp.sum(jnp.where(diagonal, level, 0.0), axis=0, keepdims=True)
    over = owed[:, 0:1] - level
    shortfall[...] = jnp.sum(jnp.where(diagonal, over, 0.0), axis=0, keepdims=True)

    def sent(r, carry):
        for h in range(2):
            for j in range(1, 4):
                pass_loss(r, h, j).wait_send()
                pass_row(r, h, j).wait_send()

        @pl.when(r < CHUNKS)
        def _():
            for s in range(2):
                scatter_one(r, s).wait_send()
                scatter_two(r, s).wait_send()
                gather_one(r, s, second[s]).wait_send()
                gather_two(r, s, first[s]).wait_send()
            give_sibling(r, c).wait_send()

        return carry

    lax.fori_loop(0, CHUNKS + 1, sent, 0)


def hand_over(*refs):
    for array, result in zip(refs[:3], refs[3:]):
        result[...] = array[...]


def local(history, block_starts, block_lengths, vol_scale, exposure, realized):
    own_days, width = history.shape
    paths = block_starts.shape[0]
    accounts = exposure.shape[0]
    mine = accounts // 16
    q, r = CHUNKS, CHUNKS + 1
    half = paths // q // 2
    block = half // 8
    vmem = pl.BlockSpec(memory_space=pltpu.VMEM)
    raw = pl.BlockSpec(memory_space=pl.ANY)
    bf16, f32 = jnp.bfloat16, jnp.float32
    dma = pltpu.SemaphoreType.DMA
    results = (
        jax.ShapeDtypeStruct((mine, paths), bf16),
        jax.ShapeDtypeStruct((1, mine), f32),
        jax.ShapeDtypeStruct((1, mine), f32),
    )
    found = pl.pallas_call(
        kernel,
        out_shape=results,
        in_specs=[raw, vmem, vmem, vmem, raw, vmem],
        out_specs=(vmem, vmem, vmem),
        scratch_shapes=[
            pltpu.VMEM((2, own_days, width), bf16),
            pltpu.VMEM((accounts, width), bf16),
            pltpu.VMEM((q, half, 2 * own_days), bf16),
            pltpu.VMEM((q, 2, 2, 2 * block, width), bf16),
            pltpu.VMEM((q, 2, 2 * block, width), bf16),
            pltpu.VMEM((q, 2, 2, block, width), bf16),
            pltpu.VMEM((q, 2, block, width), bf16),
            pltpu.VMEM((r, 2, 2, 2, 2, block, width), bf16),
            pltpu.VMEM((r, 2, 4, 4, mine, half), bf16),
            pltpu.VMEM((r, 2, 3, 4, mine, half), bf16),
            pltpu.VMEM((r, 2, 4, mine, half), bf16),
            pltpu.VMEM((r, 2, 3, mine, half), bf16),
            pltpu.VMEM((mine, half), f32),
            pltpu.VMEM((mine, half), f32),
            dma((2,)),
            dma,
            dma,
            dma((4, 2, q)),
            dma((4, 2, q)),
            dma((q,)),
            dma((q,)),
            dma((2, 2, 3, r)),
            dma((2, 2, 3, r)),
        ],
        compiler_params=pltpu.CompilerParams(
            collective_id=0, has_side_effects=True, vmem_limit_bytes=60 << 20
        ),
        name="backtest",
    )(history, block_starts.T, block_lengths.T, vol_scale.reshape(1, width), exposure, realized)
    out, margin, shortfall = pl.pallas_call(
        hand_over,
        out_shape=results,
        in_specs=[vmem] * 3,
        out_specs=(vmem,) * 3,
        name="results",
    )(*found)
    return out, margin.reshape(mine), shortfall.reshape(mine)


def solution(mesh):
    in_specs = (P("days", "fac"), P(), P(), P("fac"), P("days", "fac"), P("fac"))
    out_specs = (P(("days", "fac"), None), P(("days", "fac")), P(("days", "fac")))
    return jax.shard_map(local, mesh=mesh, in_specs=in_specs, out_specs=out_specs, check_vma=False)
```

```python
import functools

import jax
import jax.numpy as jnp
from jax import lax
from jax.experimental import pallas as pl
from jax.experimental.pallas import tpu as pltpu
from jax.sharding import PartitionSpec as P

CHUNKS = 16
PAIRS, CHIPS, SPREAD, CROSS, REVALUE, FOLD, FINISH = 3, 5, 7, 9, 9, 12, 14
DEEP = 4


def bits(place):
    return (place % 2 + place // 2) % 2, place // 2


def remote(src, dst, send, recv, device):
    return pltpu.make_async_remote_copy(
        src_ref=src,
        dst_ref=dst,
        send_sem=send,
        recv_sem=recv,
        device_id=device,
        device_id_type=pl.DeviceIdType.MESH,
    )


def kernel(
    hist, starts, lens, vol, expo, real,
    out, margin, shortfall,
    days, book, table, counts, part, part_in, pair, pair_in, shock,
    loss, loss_in, row, row_in, sums, owed,
    here, days_send, days_recv, x_send, x_recv, sib_send, sib_recv, f_send, f_recv,
):
    own_days, width = hist.shape
    paths = starts.shape[1]
    d = lax.axis_index("days")
    f = lax.axis_index("fac")
    x, c = d // 2, d % 2
    y, z = f // 4, f % 4
    u, v = bits(x)
    sibling = {"days": x * 2 + 1 - c}
    over_u = {"days": (x + 1 - 2 * (x % 2)) * 2 + c}
    over_v = {"days": (3 - x) * 2 + c}
    over_y = [{"fac": (y + j) % 4 * 4 + z} for j in range(1, 4)]
    over_z = [{"fac": y * 4 + (z + j) % 4} for j in range(1, 4)]
    first, second = (u, v), (v, u)
    over_first, over_second = (over_u, over_v), (over_v, over_u)
    place = ((z, y), (y, z))
    over_place = ((over_z, over_y), (over_y, over_z))

    load_book = pltpu.make_async_copy(expo, book, here.at[0])
    load_days = pltpu.make_async_copy(hist, days.at[c], here.at[1])
    load_days.start()
    load_book.start()
    barrier = pltpu.get_barrier_semaphore()
    everyone = (sibling, over_u, over_v, *over_y, *over_z)
    for device in everyone:
        pl.semaphore_signal(barrier, inc=1, device_id=device, device_id_type=pl.DeviceIdType.MESH)
    pl.semaphore_wait(barrier, len(everyone))

    share_days = remote(hist, days.at[c], days_send, days_recv, sibling)
    share_days.start()

    shock[0] = jnp.zeros(shock.shape[1:], shock.dtype)
    lead = shock.shape[4]
    rows = lax.broadcasted_iota(jnp.int32, (lead, width), 0)
    moved = jnp.broadcast_to(-real[...].astype(jnp.float32).reshape(1, width), (lead, width))
    shock[0, 0, 0, 0] = jnp.where(rows == 0, moved, 0.0).astype(shock.dtype)
    sums[...] = jnp.zeros_like(sums)

    half = paths // CHUNKS // 2
    wide = width // 2
    chip_days = 2 * own_days
    mine = out.shape[0]

    def count_days(q):
        at = (q * 2 + c) * half
        lanes = pl.ds(pl.multiple_of(at // 128 * 128, 128), 128)
        low = starts[:, lanes]
        both = jnp.concatenate([low, low + lens[:, lanes]], axis=0).astype(jnp.float32)
        table[...] = jnp.concatenate([both] * 16, axis=0).T
        day = (lax.broadcasted_iota(jnp.int32, (16, chip_days), 1) + x * chip_days).astype(jnp.float32)
        for group in range(half // 16):
            piece = table[pl.ds(pl.multiple_of(at % 128 + group * 16, 16), 16), :]
            total = jnp.zeros((16, chip_days), jnp.float32)
            for block in range(4):
                inside = (day >= piece[:, block : block + 1]) & (day < piece[:, block + 4 : block + 5])
                total = total + jnp.where(inside, 1.0, 0.0)
            counts[q, group * 16 : group * 16 + 16, :] = total.astype(counts.dtype)

    count_days(0)
    count_days(1)
    load_days.wait()
    share_days.wait()

    def scatter_one(q, s):
        theirs = part.at[q, 1, :, 1 - v] if s else part.at[q, 0, 1 - u]
        return remote(theirs, part_in.at[q, s], x_send.at[0, s, q % DEEP], x_recv.at[0, s, q], over_first[s])

    def scatter_two(q, s):
        theirs = pair.at[q, s, 1 - second[s]]
        return remote(theirs, pair_in.at[q, s], x_send.at[1, s, q % DEEP], x_recv.at[1, s, q], over_second[s])

    def gather_one(q, s, own=True):
        b = second[s] if own else 1 - second[s]
        rows = shock.at[q + 1, c, b, v, :, wide:] if s else shock.at[q + 1, c, u, b, :, :wide]
        return remote(rows, rows, x_send.at[2, s, q % DEEP], x_recv.at[2, s, q], over_second[s])

    def gather_two(q, s, own=True):
        b = first[s] if own else 1 - first[s]
        rows = shock.at[q + 1, c, :, b, :, wide:] if s else shock.at[q + 1, c, b, :, :, :wide]
        return remote(rows, rows, x_send.at[3, s, q % DEEP], x_recv.at[3, s, q], over_first[s])

    def give_sibling(q, own=True):
        rows = shock.at[q + 1, c if own else 1 - c]
        return remote(rows, rows, sib_send.at[q % DEEP], sib_recv.at[q], sibling)

    def pass_loss(r, h, j):
        return remote(
            loss.at[r, h, (place[h][0] + j) % 4], loss_in.at[r, h, j - 1],
            f_send.at[0, h, j - 1, r % DEEP], f_recv.at[0, h, j - 1, r], over_place[h][0][j - 1],
        )

    def pass_row(r, h, j):
        return remote(
            row.at[r, h, (place[h][1] + j) % 4], row_in.at[r, h, j - 1],
            f_send.at[1, h, j - 1, r % DEEP], f_recv.at[1, h, j - 1, r], over_place[h][1][j - 1],
        )

    def launch(copy, q, *which):
        @pl.when(q >= DEEP)
        def _():
            copy(q - DEEP, *which).wait_send()

        copy(q, *which).start()

    def stage(turn, count, body):
        @pl.when((turn >= 0) & (turn < count))
        def _():
            body(turn)

    def sum_days(q):
        whole = days[...].reshape(chip_days, width)
        both = counts[pl.ds(q, 2)].reshape(2 * half, chip_days)
        total = jnp.dot(both, whole, preferred_element_type=jnp.float32).astype(part.dtype)
        for i in range(2):
            for s in range(2):
                own = total[i * half : i * half + half, s * wide : s * wide + wide]
                part[q + i, s] = own.reshape(part.shape[2:])
        for i in range(2):
            for s in range(2):
                launch(scatter_one, q + i, s)

    def sum_pairs(q):
        for s in range(2):
            scatter_one(q, s).wait_recv()
            kept = part[q, 1, :, v] if s else part[q, 0, u]
            total = kept.astype(jnp.float32) + part_in[q, s].astype(jnp.float32)
            pair[q, s] = total.astype(pair.dtype)
            launch(scatter_two, q, s)

    def sum_chips(q):
        for s in range(2):
            scatter_two(q, s).wait_recv()
            total = pair[q, s, second[s]].astype(jnp.float32) + pair_in[q, s].astype(jnp.float32)
            scaled = total * -vol[:, s * wide : s * wide + wide]
            shock[q + 1, c, u, v, :, s * wide : s * wide + wide] = scaled.astype(shock.dtype)
            launch(gather_one, q, s)

    def spread(q):
        for s in range(2):
            gather_one(q, s, False).wait_recv()
            launch(gather_two, q, s)

    def cross(q):
        for s in range(2):
            gather_two(q, s, False).wait_recv()
        launch(give_sibling, q)

    def revalue(r):
        @pl.when(r == 0)
        def _():
            load_book.wait()

        @pl.when(r > 0)
        def _():
            give_sibling(r - 1, False).wait_recv()

        moves = shock[r].reshape(2 * half, width)
        value = lax.dot_general(
            book[...], moves, (((1,), (1,)), ((), ())), preferred_element_type=jnp.float32
        ).astype(loss.dtype)
        few = mine // 2
        for h in range(2):
            for owner in range(16):
                at = (owner // 4, owner % 4) if h else (owner % 4, owner // 4)
                top = owner * mine + h * few
                loss[r, h, at[0], at[1]] = value[top : top + few]
        for h in range(2):
            for j in range(1, 4):
                launch(pass_loss, r, h, j)

    def fold(r):
        for h in range(2):
            total = loss[r, h, place[h][0]].astype(jnp.float32)
            for j in range(1, 4):
                pass_loss(r, h, j).wait_recv()
                total = total + loss_in[r, h, j - 1].astype(jnp.float32)
            row[r, h] = total.astype(row.dtype)
            for j in range(1, 4):
                launch(pass_row, r, h, j)

    def finish(r):
        few = mine // 2
        for h in range(2):
            total = row[r, h, place[h][1]].astype(jnp.float32)
            for j in range(1, 4):
                pass_row(r, h, j).wait_recv()
                total = total + row_in[r, h, j - 1].astype(jnp.float32)

            @pl.when(r > 0)
            def _():
                at = pl.multiple_of((r - 1) * 2 * half, 2 * half)
                out[h * few : h * few + few, pl.ds(at, 2 * half)] = total.astype(out.dtype)
                sums[h * few : h * few + few, :] = sums[h * few : h * few + few, :] + jnp.exp(total)

            @pl.when(r == 0)
            def _():
                owed[h * few : h * few + few, :] = total

    def turn(t, carry):
        stage(t - PAIRS, CHUNKS, sum_pairs)
        stage(t - CHIPS, CHUNKS, sum_chips)
        stage(t - SPREAD, CHUNKS, spread)
        stage(t - CROSS, CHUNKS, cross)
        stage(jnp.where(t % 2 == 0, t, -1), CHUNKS, sum_days)
        stage(t + 2, CHUNKS, count_days)
        stage(t - REVALUE, CHUNKS + 1, revalue)
        stage(t - FOLD, CHUNKS + 1, fold)
        stage(t - FINISH, CHUNKS + 1, finish)
        return carry

    lax.fori_loop(0, CHUNKS + 1 + FINISH, turn, 0)

    level = jnp.log(jnp.sum(sums[...], axis=1, keepdims=True) * (1.0 / paths))
    diagonal = lax.broadcasted_iota(jnp.int32, (mine, mine), 0) == lax.broadcasted_iota(
        jnp.int32, (mine, mine), 1
    )
    margin[...] = jnp.sum(jnp.where(diagonal, level, 0.0), axis=0, keepdims=True)
    over = owed[:, 0:1] - level
    shortfall[...] = jnp.sum(jnp.where(diagonal, over, 0.0), axis=0, keepdims=True)

    def sent(i, carry):
        for h in range(2):
            for j in range(1, 4):
                pass_loss(CHUNKS - i, h, j).wait_send()
                pass_row(CHUNKS - i, h, j).wait_send()
        for s in range(2):
            for copy in (scatter_one, scatter_two, gather_one, gather_two):
                copy(CHUNKS - 1 - i, s).wait_send()
        give_sibling(CHUNKS - 1 - i).wait_send()
        return carry

    lax.fori_loop(0, DEEP, sent, 0)


def hand_over(*refs):
    for array, result in zip(refs[:3], refs[3:]):
        result[...] = array[...]


def local(history, block_starts, block_lengths, vol_scale, exposure, realized):
    own_days, width = history.shape
    paths = block_starts.shape[0]
    accounts = exposure.shape[0]
    mine = accounts // 16
    q, r = CHUNKS, CHUNKS + 1
    half = paths // q // 2
    block, wide, few = half // 4, width // 2, mine // 2
    vmem = pl.BlockSpec(memory_space=pltpu.VMEM)
    raw = pl.BlockSpec(memory_space=pl.ANY)
    bf16, f32 = jnp.bfloat16, jnp.float32
    dma = pltpu.SemaphoreType.DMA
    results = (
        jax.ShapeDtypeStruct((mine, paths), bf16),
        jax.ShapeDtypeStruct((1, mine), f32),
        jax.ShapeDtypeStruct((1, mine), f32),
    )
    found = pl.pallas_call(
        kernel,
        out_shape=results,
        in_specs=[raw, vmem, vmem, vmem, raw, vmem],
        out_specs=(vmem, vmem, vmem),
        scratch_shapes=[
            pltpu.VMEM((2, own_days, width), bf16),
            pltpu.VMEM((accounts, width), bf16),
            pltpu.VMEM((128, 128), f32),
            pltpu.VMEM((q, half, 2 * own_days), bf16),
            pltpu.VMEM((q, 2, 2, 2, block, wide), bf16),
            pltpu.VMEM((q, 2, 2, block, wide), bf16),
            pltpu.VMEM((q, 2, 2, block, wide), bf16),
            pltpu.VMEM((q, 2, block, wide), bf16),
            pltpu.VMEM((r, 2, 2, 2, block, width), bf16),
            pltpu.VMEM((r, 2, 4, 4, few, 2 * half), bf16),
            pltpu.VMEM((r, 2, 3, 4, few, 2 * half), bf16),
            pltpu.VMEM((r, 2, 4, few, 2 * half), bf16),
            pltpu.VMEM((r, 2, 3, few, 2 * half), bf16),
            pltpu.VMEM((mine, 2 * half), f32),
            pltpu.VMEM((mine, 2 * half), f32),
            dma((2,)),
            dma,
            dma,
            dma((4, 2, DEEP)),
            dma((4, 2, q)),
            dma((DEEP,)),
            dma((q,)),
            dma((2, 2, 3, DEEP)),
            dma((2, 2, 3, r)),
        ],
        compiler_params=pltpu.CompilerParams(
            collective_id=0, has_side_effects=True, vmem_limit_bytes=60 << 20
        ),
        name="backtest",
    )(history, block_starts.T, block_lengths.T, vol_scale.reshape(1, width), exposure, realized)
    out, margin, shortfall = pl.pallas_call(
        hand_over,
        out_shape=results,
        in_specs=[vmem] * 3,
        out_specs=(vmem,) * 3,
        name="results",
    )(*found)
    return out, margin.reshape(mine), shortfall.reshape(mine)


def solution(mesh):
    in_specs = (P("days", "fac"), P(), P(), P("fac"), P("days", "fac"), P("fac"))
    out_specs = (P(("days", "fac"), None), P(("days", "fac")), P(("days", "fac")))
    return jax.shard_map(local, mesh=mesh, in_specs=in_specs, out_specs=out_specs, check_vma=False)
```

```python
import functools

import jax
import jax.numpy as jnp
from jax import lax
from jax.experimental import pallas as pl
from jax.experimental.pallas import tpu as pltpu
from jax.sharding import PartitionSpec as P

CHUNKS = 16
PAIRS, CHIPS, SPREAD, CROSS, REVALUE, FOLD, FINISH = 3, 5, 7, 9, 9, 12, 14
DEEP = 2


def bits(place):
    return (place % 2 + place // 2) % 2, place // 2


def remote(src, dst, send, recv, device):
    return pltpu.make_async_remote_copy(
        src_ref=src,
        dst_ref=dst,
        send_sem=send,
        recv_sem=recv,
        device_id=device,
        device_id_type=pl.DeviceIdType.MESH,
    )


def kernel(
    hist, starts, lens, vol, expo, real,
    out, margin, shortfall,
    days, book, table, counts, part, part_in, pair, pair_in, shock,
    loss, loss_in, row, row_in, sums, owed,
    here, days_send, days_recv, x_send, x_recv, sib_send, sib_recv, f_send, f_recv,
):
    own_days, width = hist.shape
    paths = starts.shape[1]
    d = lax.axis_index("days")
    f = lax.axis_index("fac")
    x, c = d // 2, d % 2
    y, z = f // 4, f % 4
    u, v = bits(x)
    sibling = {"days": x * 2 + 1 - c}
    over_u = {"days": (x + 1 - 2 * (x % 2)) * 2 + c}
    over_v = {"days": (3 - x) * 2 + c}
    over_y = [{"fac": (y + j) % 4 * 4 + z} for j in range(1, 4)]
    over_z = [{"fac": y * 4 + (z + j) % 4} for j in range(1, 4)]
    first, second = (u, v), (v, u)
    over_first, over_second = (over_u, over_v), (over_v, over_u)
    place = ((z, y), (y, z))
    over_place = ((over_z, over_y), (over_y, over_z))

    load_book = pltpu.make_async_copy(expo, book, here.at[0])
    load_days = pltpu.make_async_copy(hist, days.at[c], here.at[1])
    load_days.start()
    load_book.start()
    barrier = pltpu.get_barrier_semaphore()
    everyone = (sibling, over_u, over_v, *over_y, *over_z)
    for device in everyone:
        pl.semaphore_signal(barrier, inc=1, device_id=device, device_id_type=pl.DeviceIdType.MESH)
    pl.semaphore_wait(barrier, len(everyone))

    share_days = remote(hist, days.at[c], days_send, days_recv, sibling)
    share_days.start()

    shock[0] = jnp.zeros(shock.shape[1:], shock.dtype)
    lead = shock.shape[4]
    rows = lax.broadcasted_iota(jnp.int32, (lead, width), 0)
    moved = jnp.broadcast_to(-real[...].astype(jnp.float32).reshape(1, width), (lead, width))
    shock[0, 0, 0, 0] = jnp.where(rows == 0, moved, 0.0).astype(shock.dtype)
    sums[...] = jnp.zeros_like(sums)

    half = paths // CHUNKS // 2
    wide = width // 2
    chip_days = 2 * own_days
    mine = out.shape[0]

    def count_days(q):
        at = (q * 2 + c) * half
        lanes = pl.ds(pl.multiple_of(at // 128 * 128, 128), 128)
        low = starts[:, lanes]
        both = jnp.concatenate([low, low + lens[:, lanes]], axis=0).astype(jnp.float32)
        table[...] = jnp.concatenate([both] * 16, axis=0).T
        day = (lax.broadcasted_iota(jnp.int32, (16, chip_days), 1) + x * chip_days).astype(jnp.float32)
        for group in range(half // 16):
            piece = table[pl.ds(pl.multiple_of(at % 128 + group * 16, 16), 16), :]
            total = jnp.zeros((16, chip_days), jnp.float32)
            for block in range(4):
                inside = (day >= piece[:, block : block + 1]) & (day < piece[:, block + 4 : block + 5])
                total = total + jnp.where(inside, 1.0, 0.0)
            counts[q, group * 16 : group * 16 + 16, :] = total.astype(counts.dtype)

    count_days(0)
    count_days(1)
    load_days.wait()
    share_days.wait()

    def scatter_one(q, s):
        theirs = part.at[q, 1, :, 1 - v] if s else part.at[q, 0, 1 - u]
        return remote(theirs, part_in.at[q, s], x_send.at[0, q % DEEP], x_recv.at[0, q], over_first[s])

    def scatter_two(q, s):
        theirs = pair.at[q, s, 1 - second[s]]
        return remote(theirs, pair_in.at[q, s], x_send.at[1, q % DEEP], x_recv.at[1, q], over_second[s])

    def gather_one(q, s):
        b = second[s]
        rows = shock.at[q + 1, c, b, v, :, wide:] if s else shock.at[q + 1, c, u, b, :, :wide]
        return remote(rows, rows, x_send.at[2, q % DEEP], x_recv.at[2, q], over_second[s])

    def gather_two(q, s):
        b = first[s]
        rows = shock.at[q + 1, c, :, b, :, wide:] if s else shock.at[q + 1, c, b, :, :, :wide]
        return remote(rows, rows, x_send.at[3, q % DEEP], x_recv.at[3, q], over_first[s])

    def give_sibling(q, own=True):
        rows = shock.at[q + 1, c if own else 1 - c]
        return remote(rows, rows, sib_send.at[q % DEEP], sib_recv.at[q], sibling)

    def pass_loss(r, h, j):
        return remote(
            loss.at[r, h, (place[h][0] + j) % 4], loss_in.at[r, h, j - 1],
            f_send.at[0, r % DEEP], f_recv.at[0, r], over_place[h][0][j - 1],
        )

    def pass_row(r, h, j):
        return remote(
            row.at[r, h, (place[h][1] + j) % 4], row_in.at[r, h, j - 1],
            f_send.at[1, r % DEEP], f_recv.at[1, r], over_place[h][1][j - 1],
        )

    def x_copies(kind, q):
        held = part_in.at[q] if kind in (0, 3) else pair_in.at[q]
        return remote(held, held, x_send.at[kind, q % DEEP], x_recv.at[kind, q], over_u)

    def f_copies(kind, r):
        held = row_in.at[r] if kind else loss_in.at[r]
        return remote(held, held, f_send.at[kind, r % DEEP], f_recv.at[kind, r], over_z[0])

    def x_launch(kind, copy, q):
        @pl.when(q >= DEEP)
        def _():
            x_copies(kind, q - DEEP).wait_send()

        for s in range(2):
            copy(q, s).start()

    def f_launch(kind, copy, r):
        @pl.when(r >= DEEP)
        def _():
            f_copies(kind, r - DEEP).wait_send()

        for h in range(2):
            for j in range(1, 4):
                copy(r, h, j).start()

    def stage(turn, count, body):
        @pl.when((turn >= 0) & (turn < count))
        def _():
            body(turn)

    def sum_days(q):
        whole = days[...].reshape(chip_days, width)
        both = counts[pl.ds(q, 2)].reshape(2 * half, chip_days)
        total = jnp.dot(both, whole, preferred_element_type=jnp.float32).astype(part.dtype)
        for i in range(2):
            for s in range(2):
                own = total[i * half : i * half + half, s * wide : s * wide + wide]
                part[q + i, s] = own.reshape(part.shape[2:])
        for i in range(2):
            x_launch(0, scatter_one, q + i)

    def sum_pairs(q):
        x_copies(0, q).wait_recv()
        for s in range(2):
            kept = part[q, 1, :, v] if s else part[q, 0, u]
            total = kept.astype(jnp.float32) + part_in[q, s].astype(jnp.float32)
            pair[q, s] = total.astype(pair.dtype)
        x_launch(1, scatter_two, q)

    def sum_chips(q):
        x_copies(1, q).wait_recv()
        for s in range(2):
            total = pair[q, s, second[s]].astype(jnp.float32) + pair_in[q, s].astype(jnp.float32)
            scaled = total * -vol[:, s * wide : s * wide + wide]
            shock[q + 1, c, u, v, :, s * wide : s * wide + wide] = scaled.astype(shock.dtype)
        x_launch(2, gather_one, q)

    def spread(q):
        x_copies(2, q).wait_recv()
        x_launch(3, gather_two, q)

    def cross(q):
        x_copies(3, q).wait_recv()

        @pl.when(q >= DEEP)
        def _():
            give_sibling(q - DEEP).wait_send()

        give_sibling(q).start()

    def revalue(r):
        @pl.when(r == 0)
        def _():
            load_book.wait()

        @pl.when(r > 0)
        def _():
            give_sibling(r - 1, False).wait_recv()

        moves = shock[r].reshape(2 * half, width)
        value = lax.dot_general(
            book[...], moves, (((1,), (1,)), ((), ())), preferred_element_type=jnp.float32
        ).astype(loss.dtype)
        few = mine // 2
        for h in range(2):
            for owner in range(16):
                at = (owner // 4, owner % 4) if h else (owner % 4, owner // 4)
                top = owner * mine + h * few
                loss[r, h, at[0], at[1]] = value[top : top + few]
        f_launch(0, pass_loss, r)

    def fold(r):
        f_copies(0, r).wait_recv()
        for h in range(2):
            total = loss[r, h, place[h][0]].astype(jnp.float32)
            for j in range(1, 4):
                total = total + loss_in[r, h, j - 1].astype(jnp.float32)
            row[r, h] = total.astype(row.dtype)
        f_launch(1, pass_row, r)

    def finish(r):
        few = mine // 2
        f_copies(1, r).wait_recv()
        for h in range(2):
            total = row[r, h, place[h][1]].astype(jnp.float32)
            for j in range(1, 4):
                total = total + row_in[r, h, j - 1].astype(jnp.float32)

            @pl.when(r > 0)
            def _():
                at = pl.multiple_of((r - 1) * 2 * half, 2 * half)
                out[h * few : h * few + few, pl.ds(at, 2 * half)] = total.astype(out.dtype)
                sums[h * few : h * few + few, :] = sums[h * few : h * few + few, :] + jnp.exp(total)

            @pl.when(r == 0)
            def _():
                owed[h * few : h * few + few, :] = total

    def turn(t, carry):
        stage(t - PAIRS, CHUNKS, sum_pairs)
        stage(t - CHIPS, CHUNKS, sum_chips)
        stage(t - SPREAD, CHUNKS, spread)
        stage(t - CROSS, CHUNKS, cross)
        stage(jnp.where(t % 2 == 0, t, -1), CHUNKS, sum_days)
        stage(t + 2, CHUNKS, count_days)
        stage(t - REVALUE, CHUNKS + 1, revalue)
        stage(t - FOLD, CHUNKS + 1, fold)
        stage(t - FINISH, CHUNKS + 1, finish)
        return carry

    lax.fori_loop(0, CHUNKS + 1 + FINISH, turn, 0)

    level = jnp.log(jnp.sum(sums[...], axis=1, keepdims=True) * (1.0 / paths))
    diagonal = lax.broadcasted_iota(jnp.int32, (mine, mine), 0) == lax.broadcasted_iota(
        jnp.int32, (mine, mine), 1
    )
    margin[...] = jnp.sum(jnp.where(diagonal, level, 0.0), axis=0, keepdims=True)
    over = owed[:, 0:1] - level
    shortfall[...] = jnp.sum(jnp.where(diagonal, over, 0.0), axis=0, keepdims=True)

    def sent(i, carry):
        for kind in range(2):
            f_copies(kind, CHUNKS - i).wait_send()
        for kind in range(4):
            x_copies(kind, CHUNKS - 1 - i).wait_send()
        give_sibling(CHUNKS - 1 - i).wait_send()
        return carry

    lax.fori_loop(0, DEEP, sent, 0)


def hand_over(*refs):
    for array, result in zip(refs[:3], refs[3:]):
        result[...] = array[...]


def local(history, block_starts, block_lengths, vol_scale, exposure, realized):
    own_days, width = history.shape
    paths = block_starts.shape[0]
    accounts = exposure.shape[0]
    mine = accounts // 16
    q, r = CHUNKS, CHUNKS + 1
    half = paths // q // 2
    block, wide, few = half // 4, width // 2, mine // 2
    vmem = pl.BlockSpec(memory_space=pltpu.VMEM)
    raw = pl.BlockSpec(memory_space=pl.ANY)
    bf16, f32 = jnp.bfloat16, jnp.float32
    dma = pltpu.SemaphoreType.DMA
    results = (
        jax.ShapeDtypeStruct((mine, paths), bf16),
        jax.ShapeDtypeStruct((1, mine), f32),
        jax.ShapeDtypeStruct((1, mine), f32),
    )
    found = pl.pallas_call(
        kernel,
        out_shape=results,
        in_specs=[raw, vmem, vmem, vmem, raw, vmem],
        out_specs=(vmem, vmem, vmem),
        scratch_shapes=[
            pltpu.VMEM((2, own_days, width), bf16),
            pltpu.VMEM((accounts, width), bf16),
            pltpu.VMEM((128, 128), f32),
            pltpu.VMEM((q, half, 2 * own_days), bf16),
            pltpu.VMEM((q, 2, 2, 2, block, wide), bf16),
            pltpu.VMEM((q, 2, 2, block, wide), bf16),
            pltpu.VMEM((q, 2, 2, block, wide), bf16),
            pltpu.VMEM((q, 2, block, wide), bf16),
            pltpu.VMEM((r, 2, 2, 2, block, width), bf16),
            pltpu.VMEM((r, 2, 4, 4, few, 2 * half), bf16),
            pltpu.VMEM((r, 2, 3, 4, few, 2 * half), bf16),
            pltpu.VMEM((r, 2, 4, few, 2 * half), bf16),
            pltpu.VMEM((r, 2, 3, few, 2 * half), bf16),
            pltpu.VMEM((mine, 2 * half), f32),
            pltpu.VMEM((mine, 2 * half), f32),
            dma((2,)),
            dma,
            dma,
            dma((4, DEEP)),
            dma((4, q)),
            dma((DEEP,)),
            dma((q,)),
            dma((2, DEEP)),
            dma((2, r)),
        ],
        compiler_params=pltpu.CompilerParams(
            collective_id=0, has_side_effects=True, vmem_limit_bytes=60 << 20
        ),
        name="backtest",
    )(history, block_starts.T, block_lengths.T, vol_scale.reshape(1, width), exposure, realized)
    out, margin, shortfall = pl.pallas_call(
        hand_over,
        out_shape=results,
        in_specs=[vmem] * 3,
        out_specs=(vmem,) * 3,
        name="results",
    )(*found)
    return out, margin.reshape(mine), shortfall.reshape(mine)


def solution(mesh):
    in_specs = (P("days", "fac"), P(), P(), P("fac"), P("days", "fac"), P("fac"))
    out_specs = (P(("days", "fac"), None), P(("days", "fac")), P(("days", "fac")))
    return jax.shard_map(local, mesh=mesh, in_specs=in_specs, out_specs=out_specs, check_vma=False)
```

```python
import functools

import jax
import jax.numpy as jnp
from jax import lax
from jax.experimental import pallas as pl
from jax.experimental.pallas import tpu as pltpu
from jax.sharding import PartitionSpec as P

CHUNKS = 16
PAIRS, CHIPS, SPREAD, CROSS, REVALUE, FOLD, FINISH = 3, 5, 7, 9, 9, 12, 14
DEEP = 2
FAR = 8


def bits(place):
    return (place % 2 + place // 2) % 2, place // 2


def remote(src, dst, send, recv, device):
    return pltpu.make_async_remote_copy(
        src_ref=src,
        dst_ref=dst,
        send_sem=send,
        recv_sem=recv,
        device_id=device,
        device_id_type=pl.DeviceIdType.MESH,
    )


def kernel(
    hist, starts, lens, vol, expo, real,
    out, margin, shortfall,
    days, book, table, counts, part, part_in, pair, pair_in, shock,
    loss, loss_in, row, row_in, sums, owed,
    here, days_send, days_recv, x_send, x_recv, sib_send, sib_recv, f_send, f_recv,
):
    own_days, width = hist.shape
    paths = starts.shape[1]
    d = lax.axis_index("days")
    f = lax.axis_index("fac")
    x, c = d // 2, d % 2
    y, z = f // 4, f % 4
    u, v = bits(x)
    sibling = {"days": x * 2 + 1 - c}
    over_u = {"days": (x + 1 - 2 * (x % 2)) * 2 + c}
    over_v = {"days": (3 - x) * 2 + c}
    over_y = [{"fac": (y + j) % 4 * 4 + z} for j in range(1, 4)]
    over_z = [{"fac": y * 4 + (z + j) % 4} for j in range(1, 4)]
    first, second = (u, v), (v, u)
    over_first, over_second = (over_u, over_v), (over_v, over_u)
    place = ((z, y), (y, z))
    over_place = ((over_z, over_y), (over_y, over_z))

    load_book = pltpu.make_async_copy(expo, book, here.at[0])
    load_days = pltpu.make_async_copy(hist, days.at[c], here.at[1])
    load_days.start()
    load_book.start()
    barrier = pltpu.get_barrier_semaphore()
    everyone = (sibling, over_u, over_v, *over_y, *over_z)
    for device in everyone:
        pl.semaphore_signal(barrier, inc=1, device_id=device, device_id_type=pl.DeviceIdType.MESH)
    pl.semaphore_wait(barrier, len(everyone))

    wide = width // 2
    share_days = []
    for s in range(2):
        columns = pl.ds(s * wide, wide)
        share_days.append(
            remote(hist.at[:, columns], days.at[c, :, columns], days_send.at[s], days_recv.at[s], sibling)
        )
        share_days[s].start()

    shock[0] = jnp.zeros(shock.shape[1:], shock.dtype)
    lead = shock.shape[4]
    rows = lax.broadcasted_iota(jnp.int32, (lead, width), 0)
    moved = jnp.broadcast_to(-real[...].astype(jnp.float32).reshape(1, width), (lead, width))
    shock[0, 0, 0, 0] = jnp.where(rows == 0, moved, 0.0).astype(shock.dtype)
    sums[...] = jnp.zeros_like(sums)

    half = paths // CHUNKS // 2
    chip_days = 2 * own_days
    mine = out.shape[0]

    def count_days(q):
        at = (q * 2 + c) * half
        lanes = pl.ds(pl.multiple_of(at // 128 * 128, 128), 128)
        low = starts[:, lanes]
        both = jnp.concatenate([low, low + lens[:, lanes]], axis=0).astype(jnp.float32)
        table[...] = jnp.concatenate([both] * 16, axis=0).T
        day = (lax.broadcasted_iota(jnp.int32, (16, chip_days), 1) + x * chip_days).astype(jnp.float32)
        for group in range(half // 16):
            piece = table[pl.ds(pl.multiple_of(at % 128 + group * 16, 16), 16), :]
            total = jnp.zeros((16, chip_days), jnp.float32)
            for block in range(4):
                inside = (day >= piece[:, block : block + 1]) & (day < piece[:, block + 4 : block + 5])
                total = total + jnp.where(inside, 1.0, 0.0)
            counts[q, group * 16 : group * 16 + 16, :] = total.astype(counts.dtype)

    count_days(0)
    count_days(1)
    load_days.wait()

    def scatter_one(q, s):
        theirs = part.at[q, 1, :, 1 - v] if s else part.at[q, 0, 1 - u]
        return remote(theirs, part_in.at[q, s], x_send.at[0, q % DEEP], x_recv.at[0, q % FAR], over_first[s])

    def scatter_two(q, s):
        theirs = pair.at[q, s, 1 - second[s]]
        return remote(theirs, pair_in.at[q, s], x_send.at[1, q % DEEP], x_recv.at[1, q % FAR], over_second[s])

    def gather_one(q, s):
        b = second[s]
        rows = shock.at[q + 1, c, b, v, :, wide:] if s else shock.at[q + 1, c, u, b, :, :wide]
        return remote(rows, rows, x_send.at[2, q % DEEP], x_recv.at[2, q % FAR], over_second[s])

    def gather_two(q, s):
        b = first[s]
        rows = shock.at[q + 1, c, :, b, :, wide:] if s else shock.at[q + 1, c, b, :, :, :wide]
        return remote(rows, rows, x_send.at[3, q % DEEP], x_recv.at[3, q % FAR], over_first[s])

    def give_sibling(q, own=True):
        rows = shock.at[q + 1, c if own else 1 - c]
        return remote(rows, rows, sib_send.at[q % DEEP], sib_recv.at[q % FAR], sibling)

    def pass_loss(r, h, j):
        return remote(
            loss.at[r, h, (place[h][0] + j) % 4], loss_in.at[r, h, j - 1],
            f_send.at[0, r % DEEP], f_recv.at[0, r % FAR], over_place[h][0][j - 1],
        )

    def pass_row(r, h, j):
        return remote(
            row.at[r, h, (place[h][1] + j) % 4], row_in.at[r, h, j - 1],
            f_send.at[1, r % DEEP], f_recv.at[1, r % FAR], over_place[h][1][j - 1],
        )

    def x_copies(kind, q):
        held = part_in.at[q] if kind in (0, 3) else pair_in.at[q]
        return remote(held, held, x_send.at[kind, q % DEEP], x_recv.at[kind, q % FAR], over_u)

    def f_copies(kind, r):
        held = row_in.at[r] if kind else loss_in.at[r]
        return remote(held, held, f_send.at[kind, r % DEEP], f_recv.at[kind, r % FAR], over_z[0])

    def x_launch(kind, copy, q):
        @pl.when(q >= DEEP)
        def _():
            x_copies(kind, q - DEEP).wait_send()

        for s in range(2):
            copy(q, s).start()

    def f_launch(kind, copy, r):
        @pl.when(r >= DEEP)
        def _():
            f_copies(kind, r - DEEP).wait_send()

        for j in (2, 1, 3):
            for h in range(2):
                copy(r, h, j).start()

    def stage(turn, count, body):
        @pl.when((turn >= 0) & (turn < count))
        def _():
            body(turn)

    def sum_days(q):
        @pl.when(q >= DEEP)
        def _():
            for i in range(2):
                x_copies(0, q + i - DEEP).wait_send()

        both = counts[pl.ds(q, 2)].reshape(2 * half, chip_days)
        for s in range(2):

            @pl.when(q == 0)
            def _():
                share_days[s].wait()

            columns = slice(s * wide, s * wide + wide)
            whole = days[:, :, columns].reshape(chip_days, wide)
            total = jnp.dot(both, whole, preferred_element_type=jnp.float32).astype(part.dtype)
            for i in range(2):
                part[q + i, s] = total[i * half : i * half + half].reshape(part.shape[2:])
                scatter_one(q + i, s).start()

    def sum_pairs(q):
        x_copies(0, q).wait_recv()
        for s in range(2):
            kept = part[q, 1, :, v] if s else part[q, 0, u]
            total = kept.astype(jnp.float32) + part_in[q, s].astype(jnp.float32)
            pair[q, s] = total.astype(pair.dtype)
        x_launch(1, scatter_two, q)

    def sum_chips(q):
        x_copies(1, q).wait_recv()
        for s in range(2):
            total = pair[q, s, second[s]].astype(jnp.float32) + pair_in[q, s].astype(jnp.float32)
            scaled = total * -vol[:, s * wide : s * wide + wide]
            shock[q + 1, c, u, v, :, s * wide : s * wide + wide] = scaled.astype(shock.dtype)
        x_launch(2, gather_one, q)

    def spread(q):
        x_copies(2, q).wait_recv()
        x_launch(3, gather_two, q)

    def cross(q):
        x_copies(3, q).wait_recv()

        @pl.when(q >= DEEP)
        def _():
            give_sibling(q - DEEP).wait_send()

        give_sibling(q).start()

    def revalue(r):
        @pl.when(r == 0)
        def _():
            load_book.wait()

        @pl.when(r > 0)
        def _():
            give_sibling(r - 1, False).wait_recv()

        moves = shock[r].reshape(2 * half, width)
        value = lax.dot_general(
            book[...], moves, (((1,), (1,)), ((), ())), preferred_element_type=jnp.float32
        ).astype(loss.dtype)
        few = mine // 2
        for h in range(2):
            for owner in range(16):
                at = (owner // 4, owner % 4) if h else (owner % 4, owner // 4)
                top = owner * mine + h * few
                loss[r, h, at[0], at[1]] = value[top : top + few]
        f_launch(0, pass_loss, r)

    def fold(r):
        f_copies(0, r).wait_recv()
        for h in range(2):
            total = loss[r, h, place[h][0]].astype(jnp.float32)
            for j in range(1, 4):
                total = total + loss_in[r, h, j - 1].astype(jnp.float32)
            row[r, h] = total.astype(row.dtype)
        f_launch(1, pass_row, r)

    def finish(r):
        few = mine // 2
        f_copies(1, r).wait_recv()
        for h in range(2):
            total = row[r, h, place[h][1]].astype(jnp.float32)
            for j in range(1, 4):
                total = total + row_in[r, h, j - 1].astype(jnp.float32)

            @pl.when(r > 0)
            def _():
                at = pl.multiple_of((r - 1) * 2 * half, 2 * half)
                out[h * few : h * few + few, pl.ds(at, 2 * half)] = total.astype(out.dtype)
                sums[h * few : h * few + few, :] = sums[h * few : h * few + few, :] + jnp.exp(total)

            @pl.when(r == 0)
            def _():
                owed[h * few : h * few + few, :] = total

    def turn(t, carry):
        stage(t - PAIRS, CHUNKS, sum_pairs)
        stage(t - CHIPS, CHUNKS, sum_chips)
        stage(t - SPREAD, CHUNKS, spread)
        stage(t - CROSS, CHUNKS, cross)
        stage(jnp.where(t % 2 == 0, t, -1), CHUNKS, sum_days)
        stage(t + 2, CHUNKS, count_days)
        stage(t - REVALUE, CHUNKS + 1, revalue)
        stage(t - FOLD, CHUNKS + 1, fold)
        stage(t - FINISH, CHUNKS + 1, finish)
        return carry

    lax.fori_loop(0, CHUNKS + 1 + FINISH, turn, 0)

    level = jnp.log(jnp.sum(sums[...], axis=1, keepdims=True) * (1.0 / paths))
    diagonal = lax.broadcasted_iota(jnp.int32, (mine, mine), 0) == lax.broadcasted_iota(
        jnp.int32, (mine, mine), 1
    )
    margin[...] = jnp.sum(jnp.where(diagonal, level, 0.0), axis=0, keepdims=True)
    over = owed[:, 0:1] - level
    shortfall[...] = jnp.sum(jnp.where(diagonal, over, 0.0), axis=0, keepdims=True)

    def sent(i, carry):
        for kind in range(2):
            f_copies(kind, CHUNKS - i).wait_send()
        for kind in range(4):
            x_copies(kind, CHUNKS - 1 - i).wait_send()
        give_sibling(CHUNKS - 1 - i).wait_send()
        return carry

    lax.fori_loop(0, DEEP, sent, 0)


def hand_over(*refs):
    for array, result in zip(refs[:3], refs[3:]):
        result[...] = array[...]


def local(history, block_starts, block_lengths, vol_scale, exposure, realized):
    own_days, width = history.shape
    paths = block_starts.shape[0]
    accounts = exposure.shape[0]
    mine = accounts // 16
    q, r = CHUNKS, CHUNKS + 1
    half = paths // q // 2
    block, wide, few = half // 4, width // 2, mine // 2
    vmem = pl.BlockSpec(memory_space=pltpu.VMEM)
    raw = pl.BlockSpec(memory_space=pl.ANY)
    bf16, f32 = jnp.bfloat16, jnp.float32
    dma = pltpu.SemaphoreType.DMA
    results = (
        jax.ShapeDtypeStruct((mine, paths), bf16),
        jax.ShapeDtypeStruct((1, mine), f32),
        jax.ShapeDtypeStruct((1, mine), f32),
    )
    found = pl.pallas_call(
        kernel,
        out_shape=results,
        in_specs=[raw, vmem, vmem, vmem, raw, vmem],
        out_specs=(vmem, vmem, vmem),
        scratch_shapes=[
            pltpu.VMEM((2, own_days, width), bf16),
            pltpu.VMEM((accounts, width), bf16),
            pltpu.VMEM((128, 128), f32),
            pltpu.VMEM((q, half, 2 * own_days), bf16),
            pltpu.VMEM((q, 2, 2, 2, block, wide), bf16),
            pltpu.VMEM((q, 2, 2, block, wide), bf16),
            pltpu.VMEM((q, 2, 2, block, wide), bf16),
            pltpu.VMEM((q, 2, block, wide), bf16),
            pltpu.VMEM((r, 2, 2, 2, block, width), bf16),
            pltpu.VMEM((r, 2, 4, 4, few, 2 * half), bf16),
            pltpu.VMEM((r, 2, 3, 4, few, 2 * half), bf16),
            pltpu.VMEM((r, 2, 4, few, 2 * half), bf16),
            pltpu.VMEM((r, 2, 3, few, 2 * half), bf16),
            pltpu.VMEM((mine, 2 * half), f32),
            pltpu.VMEM((mine, 2 * half), f32),
            dma((2,)),
            dma((2,)),
            dma((2,)),
            dma((4, DEEP)),
            dma((4, FAR)),
            dma((DEEP,)),
            dma((FAR,)),
            dma((2, DEEP)),
            dma((2, FAR)),
        ],
        compiler_params=pltpu.CompilerParams(
            collective_id=0, has_side_effects=True, vmem_limit_bytes=60 << 20
        ),
        name="backtest",
    )(history, block_starts.T, block_lengths.T, vol_scale.reshape(1, width), exposure, realized)
    out, margin, shortfall = pl.pallas_call(
        hand_over,
        out_shape=results,
        in_specs=[vmem] * 3,
        out_specs=(vmem,) * 3,
        name="results",
    )(*found)
    return out, margin.reshape(mine), shortfall.reshape(mine)


def solution(mesh):
    in_specs = (P("days", "fac"), P(), P(), P("fac"), P("days", "fac"), P("fac"))
    out_specs = (P(("days", "fac"), None), P(("days", "fac")), P(("days", "fac")))
    return jax.shard_map(local, mesh=mesh, in_specs=in_specs, out_specs=out_specs, check_vma=False)
```

```python
import functools

import jax
import jax.numpy as jnp
from jax import lax
from jax.experimental import pallas as pl
from jax.experimental.pallas import tpu as pltpu
from jax.sharding import PartitionSpec as P

CHUNKS = 16
PAIRS, CHIPS, SPREAD, CROSS, REVALUE, FOLD, FINISH = 3, 5, 7, 9, 9, 12, 14
DEEP = 2
FAR = 8


def bits(place):
    return (place % 2 + place // 2) % 2, place // 2


def remote(src, dst, send, recv, device):
    return pltpu.make_async_remote_copy(
        src_ref=src,
        dst_ref=dst,
        send_sem=send,
        recv_sem=recv,
        device_id=device,
        device_id_type=pl.DeviceIdType.MESH,
    )


def kernel(
    hist, starts, lens, vol, expo, real,
    out, margin, shortfall,
    days, book, table, counts, part, part_in, pair, pair_in, shock,
    loss, loss_in, row, row_in, sums, owed, held,
    here, leave, days_send, days_recv, x_send, x_recv, sib_send, sib_recv, f_send, f_recv,
):
    own_days, width = hist.shape
    paths = starts.shape[1]
    d = lax.axis_index("days")
    f = lax.axis_index("fac")
    x, c = d // 2, d % 2
    y, z = f // 4, f % 4
    u, v = bits(x)
    sibling = {"days": x * 2 + 1 - c}
    over_u = {"days": (x + 1 - 2 * (x % 2)) * 2 + c}
    over_v = {"days": (3 - x) * 2 + c}
    over_y = [{"fac": (y + j) % 4 * 4 + z} for j in range(1, 4)]
    over_z = [{"fac": y * 4 + (z + j) % 4} for j in range(1, 4)]
    first, second = (u, v), (v, u)
    over_first, over_second = (over_u, over_v), (over_v, over_u)
    place = ((z, y), (y, z))
    over_place = ((over_z, over_y), (over_y, over_z))

    load_book = pltpu.make_async_copy(expo, book, here.at[0])
    load_days = pltpu.make_async_copy(hist, days.at[c], here.at[1])
    load_days.start()
    load_book.start()
    barrier = pltpu.get_barrier_semaphore()
    everyone = (sibling, over_u, over_v, *over_y, *over_z)
    for device in everyone:
        pl.semaphore_signal(barrier, inc=1, device_id=device, device_id_type=pl.DeviceIdType.MESH)
    pl.semaphore_wait(barrier, len(everyone))

    wide = width // 2
    share_days = []
    for s in range(2):
        columns = pl.ds(s * wide, wide)
        share_days.append(
            remote(hist.at[:, columns], days.at[c, :, columns], days_send.at[s], days_recv.at[s], sibling)
        )
        share_days[s].start()

    shock[0] = jnp.zeros(shock.shape[1:], shock.dtype)
    lead = shock.shape[4]
    rows = lax.broadcasted_iota(jnp.int32, (lead, width), 0)
    moved = jnp.broadcast_to(-real[...].astype(jnp.float32).reshape(1, width), (lead, width))
    shock[0, 0, 0, 0] = jnp.where(rows == 0, moved, 0.0).astype(shock.dtype)
    sums[...] = jnp.zeros_like(sums)

    half = paths // CHUNKS // 2
    chip_days = 2 * own_days
    mine = out.shape[0]

    def count_days(q):
        at = (q * 2 + c) * half
        lanes = pl.ds(pl.multiple_of(at // 128 * 128, 128), 128)
        low = starts[:, lanes]
        both = jnp.concatenate([low, low + lens[:, lanes]], axis=0).astype(jnp.float32)
        table[...] = jnp.concatenate([both] * 16, axis=0).T
        day = (lax.broadcasted_iota(jnp.int32, (16, chip_days), 1) + x * chip_days).astype(jnp.float32)
        for group in range(half // 16):
            piece = table[pl.ds(pl.multiple_of(at % 128 + group * 16, 16), 16), :]
            total = jnp.zeros((16, chip_days), jnp.float32)
            for block in range(4):
                inside = (day >= piece[:, block : block + 1]) & (day < piece[:, block + 4 : block + 5])
                total = total + jnp.where(inside, 1.0, 0.0)
            counts[q, group * 16 : group * 16 + 16, :] = total.astype(counts.dtype)

    count_days(0)
    count_days(1)
    load_days.wait()

    def scatter_one(q, s):
        theirs = part.at[q, 1, :, 1 - v] if s else part.at[q, 0, 1 - u]
        return remote(theirs, part_in.at[q, s], x_send.at[0, q % DEEP], x_recv.at[0, q % FAR], over_first[s])

    def scatter_two(q, s):
        theirs = pair.at[q, s, 1 - second[s]]
        return remote(theirs, pair_in.at[q, s], x_send.at[1, q % DEEP], x_recv.at[1, q % FAR], over_second[s])

    def gather_one(q, s):
        b = second[s]
        rows = shock.at[q + 1, c, b, v, :, wide:] if s else shock.at[q + 1, c, u, b, :, :wide]
        return remote(rows, rows, x_send.at[2, q % DEEP], x_recv.at[2, q % FAR], over_second[s])

    def gather_two(q, s):
        b = first[s]
        rows = shock.at[q + 1, c, :, b, :, wide:] if s else shock.at[q + 1, c, b, :, :, :wide]
        return remote(rows, rows, x_send.at[3, q % DEEP], x_recv.at[3, q % FAR], over_first[s])

    def give_sibling(q, own=True):
        rows = shock.at[q + 1, c if own else 1 - c]
        return remote(rows, rows, sib_send.at[q % DEEP], sib_recv.at[q % FAR], sibling)

    def pass_loss(r, h, j):
        return remote(
            loss.at[r, h, (place[h][0] + j) % 4], loss_in.at[r, h, j - 1],
            f_send.at[0, r % DEEP], f_recv.at[0, r % FAR], over_place[h][0][j - 1],
        )

    def pass_row(r, h, j):
        return remote(
            row.at[r, h, (place[h][1] + j) % 4], row_in.at[r, h, j - 1],
            f_send.at[1, r % DEEP], f_recv.at[1, r % FAR], over_place[h][1][j - 1],
        )

    def x_copies(kind, q):
        held = part_in.at[q] if kind in (0, 3) else pair_in.at[q]
        return remote(held, held, x_send.at[kind, q % DEEP], x_recv.at[kind, q % FAR], over_u)

    def f_copies(kind, r):
        held = row_in.at[r] if kind else loss_in.at[r]
        return remote(held, held, f_send.at[kind, r % DEEP], f_recv.at[kind, r % FAR], over_z[0])

    def x_launch(kind, copy, q):
        @pl.when(q >= DEEP)
        def _():
            x_copies(kind, q - DEEP).wait_send()

        for s in range(2):
            copy(q, s).start()

    def f_launch(kind, copy, r):
        @pl.when(r >= DEEP)
        def _():
            f_copies(kind, r - DEEP).wait_send()

        for j in (2, 1, 3):
            for h in range(2):
                copy(r, h, j).start()

    def stage(turn, count, body):
        @pl.when((turn >= 0) & (turn < count))
        def _():
            body(turn)

    def sum_days(q):
        @pl.when(q >= DEEP)
        def _():
            for i in range(2):
                x_copies(0, q + i - DEEP).wait_send()

        both = counts[pl.ds(q, 2)].reshape(2 * half, chip_days)
        for s in range(2):

            @pl.when(q == 0)
            def _():
                share_days[s].wait()

            columns = slice(s * wide, s * wide + wide)
            whole = days[:, :, columns].reshape(chip_days, wide)
            total = jnp.dot(both, whole, preferred_element_type=jnp.float32).astype(part.dtype)
            for i in range(2):
                part[q + i, s] = total[i * half : i * half + half].reshape(part.shape[2:])
                scatter_one(q + i, s).start()

    def sum_pairs(q):
        x_copies(0, q).wait_recv()
        for s in range(2):
            kept = part[q, 1, :, v] if s else part[q, 0, u]
            total = kept.astype(jnp.float32) + part_in[q, s].astype(jnp.float32)
            pair[q, s] = total.astype(pair.dtype)
        x_launch(1, scatter_two, q)

    def sum_chips(q):
        x_copies(1, q).wait_recv()
        for s in range(2):
            total = pair[q, s, second[s]].astype(jnp.float32) + pair_in[q, s].astype(jnp.float32)
            scaled = total * -vol[:, s * wide : s * wide + wide]
            shock[q + 1, c, u, v, :, s * wide : s * wide + wide] = scaled.astype(shock.dtype)
        x_launch(2, gather_one, q)

    def spread(q):
        x_copies(2, q).wait_recv()
        x_launch(3, gather_two, q)

    def cross(q):
        x_copies(3, q).wait_recv()

        @pl.when(q >= DEEP)
        def _():
            give_sibling(q - DEEP).wait_send()

        give_sibling(q).start()

    def revalue(r):
        @pl.when(r == 0)
        def _():
            load_book.wait()

        @pl.when(r > 0)
        def _():
            give_sibling(r - 1, False).wait_recv()

        moves = shock[r].reshape(2 * half, width)
        value = lax.dot_general(
            book[...], moves, (((1,), (1,)), ((), ())), preferred_element_type=jnp.float32
        ).astype(loss.dtype)
        few = mine // 2
        for h in range(2):
            for owner in range(16):
                at = (owner // 4, owner % 4) if h else (owner % 4, owner // 4)
                top = owner * mine + h * few
                loss[r, h, at[0], at[1]] = value[top : top + few]
        f_launch(0, pass_loss, r)

    def fold(r):
        f_copies(0, r).wait_recv()
        for h in range(2):
            total = loss[r, h, place[h][0]].astype(jnp.float32)
            for j in range(1, 4):
                total = total + loss_in[r, h, j - 1].astype(jnp.float32)
            row[r, h] = total.astype(row.dtype)
        f_launch(1, pass_row, r)

    def finish(r):
        few = mine // 2
        f_copies(1, r).wait_recv()
        for h in range(2):
            total = row[r, h, place[h][1]].astype(jnp.float32)
            for j in range(1, 4):
                total = total + row_in[r, h, j - 1].astype(jnp.float32)

            @pl.when(r > 0)
            def _():
                at = pl.multiple_of((r - 1) * 2 * half, 2 * half)
                held[h * few : h * few + few, pl.ds(at, 2 * half)] = total.astype(out.dtype)
                sums[h * few : h * few + few, :] = sums[h * few : h * few + few, :] + jnp.exp(total)

            @pl.when(r == 0)
            def _():
                owed[h * few : h * few + few, :] = total

        @pl.when(r > 0)
        def _():
            lanes = pl.ds(pl.multiple_of((r - 1) * 2 * half, 2 * half), 2 * half)
            pltpu.make_async_copy(held.at[:, lanes], out.at[:, lanes], leave).start()

    def turn(t, carry):
        stage(t - PAIRS, CHUNKS, sum_pairs)
        stage(t - CHIPS, CHUNKS, sum_chips)
        stage(t - SPREAD, CHUNKS, spread)
        stage(t - CROSS, CHUNKS, cross)
        stage(jnp.where(t % 2 == 0, t, -1), CHUNKS, sum_days)
        stage(t + 2, CHUNKS, count_days)
        stage(t - REVALUE, CHUNKS + 1, revalue)
        stage(t - FOLD, CHUNKS + 1, fold)
        stage(t - FINISH, CHUNKS + 1, finish)
        return carry

    lax.fori_loop(0, CHUNKS + 1 + FINISH, turn, 0)

    level = jnp.log(jnp.sum(sums[...], axis=1, keepdims=True) * (1.0 / paths))
    diagonal = lax.broadcasted_iota(jnp.int32, (mine, mine), 0) == lax.broadcasted_iota(
        jnp.int32, (mine, mine), 1
    )
    margin[...] = jnp.sum(jnp.where(diagonal, level, 0.0), axis=0, keepdims=True)
    over = owed[:, 0:1] - level
    shortfall[...] = jnp.sum(jnp.where(diagonal, over, 0.0), axis=0, keepdims=True)

    def sent(i, carry):
        for kind in range(2):
            f_copies(kind, CHUNKS - i).wait_send()
        for kind in range(4):
            x_copies(kind, CHUNKS - 1 - i).wait_send()
        give_sibling(CHUNKS - 1 - i).wait_send()
        return carry

    lax.fori_loop(0, DEEP, sent, 0)
    pltpu.make_async_copy(held, out, leave).wait()


def hand_over(*refs):
    for array, result in zip(refs[:3], refs[3:]):
        result[...] = array[...]


def local(history, block_starts, block_lengths, vol_scale, exposure, realized):
    own_days, width = history.shape
    paths = block_starts.shape[0]
    accounts = exposure.shape[0]
    mine = accounts // 16
    q, r = CHUNKS, CHUNKS + 1
    half = paths // q // 2
    block, wide, few = half // 4, width // 2, mine // 2
    vmem = pl.BlockSpec(memory_space=pltpu.VMEM)
    raw = pl.BlockSpec(memory_space=pl.ANY)
    bf16, f32 = jnp.bfloat16, jnp.float32
    dma = pltpu.SemaphoreType.DMA
    results = (
        jax.ShapeDtypeStruct((mine, paths), bf16),
        jax.ShapeDtypeStruct((1, mine), f32),
        jax.ShapeDtypeStruct((1, mine), f32),
    )
    found = pl.pallas_call(
        kernel,
        out_shape=results,
        in_specs=[raw, vmem, vmem, vmem, raw, vmem],
        out_specs=(raw, vmem, vmem),
        scratch_shapes=[
            pltpu.VMEM((2, own_days, width), bf16),
            pltpu.VMEM((accounts, width), bf16),
            pltpu.VMEM((128, 128), f32),
            pltpu.VMEM((q, half, 2 * own_days), bf16),
            pltpu.VMEM((q, 2, 2, 2, block, wide), bf16),
            pltpu.VMEM((q, 2, 2, block, wide), bf16),
            pltpu.VMEM((q, 2, 2, block, wide), bf16),
            pltpu.VMEM((q, 2, block, wide), bf16),
            pltpu.VMEM((r, 2, 2, 2, block, width), bf16),
            pltpu.VMEM((r, 2, 4, 4, few, 2 * half), bf16),
            pltpu.VMEM((r, 2, 3, 4, few, 2 * half), bf16),
            pltpu.VMEM((r, 2, 4, few, 2 * half), bf16),
            pltpu.VMEM((r, 2, 3, few, 2 * half), bf16),
            pltpu.VMEM((mine, 2 * half), f32),
            pltpu.VMEM((mine, 2 * half), f32),
            pltpu.VMEM((mine, paths), bf16),
            dma((2,)),
            dma,
            dma((2,)),
            dma((2,)),
            dma((4, DEEP)),
            dma((4, FAR)),
            dma((DEEP,)),
            dma((FAR,)),
            dma((2, DEEP)),
            dma((2, FAR)),
        ],
        compiler_params=pltpu.CompilerParams(
            collective_id=0, has_side_effects=True, vmem_limit_bytes=60 << 20
        ),
        name="backtest",
    )(history, block_starts.T, block_lengths.T, vol_scale.reshape(1, width), exposure, realized)
    out, margin, shortfall = pl.pallas_call(
        hand_over,
        out_shape=results,
        in_specs=[vmem] * 3,
        out_specs=(vmem,) * 3,
        name="results",
    )(*found)
    return out, margin.reshape(mine), shortfall.reshape(mine)


def solution(mesh):
    in_specs = (P("days", "fac"), P(), P(), P("fac"), P("days", "fac"), P("fac"))
    out_specs = (P(("days", "fac"), None), P(("days", "fac")), P(("days", "fac")))
    return jax.shard_map(local, mesh=mesh, in_specs=in_specs, out_specs=out_specs, check_vma=False)
```

```python
import functools

import jax
import jax.numpy as jnp
from jax import lax
from jax.experimental import pallas as pl
from jax.experimental.pallas import tpu as pltpu
from jax.sharding import PartitionSpec as P

CHUNKS = 16
PAIRS, CHIPS, SPREAD, CROSS, REVALUE, FOLD, FINISH = 3, 5, 7, 9, 9, 12, 14
DEEP = 2
FAR = 8


def bits(place):
    return (place % 2 + place // 2) % 2, place // 2


def remote(src, dst, send, recv, device):
    return pltpu.make_async_remote_copy(
        src_ref=src,
        dst_ref=dst,
        send_sem=send,
        recv_sem=recv,
        device_id=device,
        device_id_type=pl.DeviceIdType.MESH,
    )


def kernel(
    hist, starts, lens, vol, expo, real,
    out, margin, shortfall,
    days, book, table, counts, part, part_in, pair, pair_in, shock,
    loss, loss_in, row, row_in, sums, owed,
    here, days_send, days_recv, x_send, x_recv, sib_send, sib_recv, f_send, f_recv,
):
    own_days, width = hist.shape
    paths = starts.shape[1]
    d = lax.axis_index("days")
    f = lax.axis_index("fac")
    x, c = d // 2, d % 2
    y, z = f // 4, f % 4
    u, v = bits(x)
    sibling = {"days": x * 2 + 1 - c}
    over_u = {"days": (x + 1 - 2 * (x % 2)) * 2 + c}
    over_v = {"days": (3 - x) * 2 + c}
    over_y = [{"fac": (y + j) % 4 * 4 + z} for j in range(1, 4)]
    over_z = [{"fac": y * 4 + (z + j) % 4} for j in range(1, 4)]
    first, second = (u, v), (v, u)
    over_first, over_second = (over_u, over_v), (over_v, over_u)
    place = ((z, y), (y, z))
    over_place = ((over_z, over_y), (over_y, over_z))

    load_book = pltpu.make_async_copy(expo, book, here.at[0])
    load_days = pltpu.make_async_copy(hist, days.at[c], here.at[1])
    load_days.start()
    load_book.start()
    barrier = pltpu.get_barrier_semaphore()
    everyone = (sibling, over_u, over_v, *over_y, *over_z)
    for device in everyone:
        pl.semaphore_signal(barrier, inc=1, device_id=device, device_id_type=pl.DeviceIdType.MESH)
    pl.semaphore_wait(barrier, len(everyone))

    wide = width // 2
    share_days = []
    for s in range(2):
        columns = pl.ds(s * wide, wide)
        share_days.append(
            remote(hist.at[:, columns], days.at[c, :, columns], days_send.at[s], days_recv.at[s], sibling)
        )
        share_days[s].start()

    shock[0] = jnp.zeros(shock.shape[1:], shock.dtype)
    lead = shock.shape[4]
    rows = lax.broadcasted_iota(jnp.int32, (lead, width), 0)
    moved = jnp.broadcast_to(-real[...].astype(jnp.float32).reshape(1, width), (lead, width))
    shock[0, 0, 0, 0] = jnp.where(rows == 0, moved, 0.0).astype(shock.dtype)
    sums[...] = jnp.zeros_like(sums)

    half = paths // CHUNKS // 2
    chip_days = 2 * own_days
    mine = out.shape[0]

    def count_days(q):
        at = (q * 2 + c) * half
        lanes = pl.ds(pl.multiple_of(at // 128 * 128, 128), 128)
        low = starts[:, lanes]
        both = jnp.concatenate([low, low + lens[:, lanes]], axis=0).astype(jnp.float32)
        table[...] = jnp.concatenate([both] * 16, axis=0).T
        day = (lax.broadcasted_iota(jnp.int32, (16, chip_days), 1) + x * chip_days).astype(jnp.float32)
        for group in range(half // 16):
            piece = table[pl.ds(pl.multiple_of(at % 128 + group * 16, 16), 16), :]
            total = jnp.zeros((16, chip_days), jnp.float32)
            for block in range(4):
                inside = (day >= piece[:, block : block + 1]) & (day < piece[:, block + 4 : block + 5])
                total = total + jnp.where(inside, 1.0, 0.0)
            counts[q, group * 16 : group * 16 + 16, :] = total.astype(counts.dtype)

    count_days(0)
    count_days(1)
    load_days.wait()

    def scatter_one(q, s):
        theirs = part.at[q, 1, :, 1 - v] if s else part.at[q, 0, 1 - u]
        return remote(theirs, part_in.at[q, s], x_send.at[0, q % DEEP], x_recv.at[0, q % FAR], over_first[s])

    def scatter_two(q, s):
        theirs = pair.at[q, s, 1 - second[s]]
        return remote(theirs, pair_in.at[q, s], x_send.at[1, q % DEEP], x_recv.at[1, q % FAR], over_second[s])

    def gather_one(q, s):
        b = second[s]
        rows = shock.at[q + 1, c, b, v, :, wide:] if s else shock.at[q + 1, c, u, b, :, :wide]
        return remote(rows, rows, x_send.at[2, q % DEEP], x_recv.at[2, q % FAR], over_second[s])

    def gather_two(q, s):
        b = first[s]
        rows = shock.at[q + 1, c, :, b, :, wide:] if s else shock.at[q + 1, c, b, :, :, :wide]
        return remote(rows, rows, x_send.at[3, q % DEEP], x_recv.at[3, q % FAR], over_first[s])

    def give_sibling(q, own=True):
        rows = shock.at[q + 1, c if own else 1 - c]
        return remote(rows, rows, sib_send.at[q % DEEP], sib_recv.at[q % FAR], sibling)

    def pass_loss(r, h, j):
        return remote(
            loss.at[r, h, (place[h][0] + j) % 4], loss_in.at[r, h, j - 1],
            f_send.at[0, r % DEEP], f_recv.at[0, r % FAR], over_place[h][0][j - 1],
        )

    def pass_row(r, h, j):
        return remote(
            row.at[r, h, (place[h][1] + j) % 4], row_in.at[r, h, j - 1],
            f_send.at[1, r % DEEP], f_recv.at[1, r % FAR], over_place[h][1][j - 1],
        )

    def x_copies(kind, q):
        held = part_in.at[q] if kind in (0, 3) else pair_in.at[q]
        return remote(held, held, x_send.at[kind, q % DEEP], x_recv.at[kind, q % FAR], over_u)

    def f_copies(kind, r):
        held = row_in.at[r] if kind else loss_in.at[r]
        return remote(held, held, f_send.at[kind, r % DEEP], f_recv.at[kind, r % FAR], over_z[0])

    def x_launch(kind, copy, q):
        @pl.when(q >= DEEP)
        def _():
            x_copies(kind, q - DEEP).wait_send()

        for s in range(2):
            copy(q, s).start()

    def f_launch(kind, copy, r):
        @pl.when(r >= DEEP)
        def _():
            f_copies(kind, r - DEEP).wait_send()

        for j in (2, 1, 3):
            for h in range(2):
                copy(r, h, j).start()

    def stage(turn, count, body):
        @pl.when((turn >= 0) & (turn < count))
        def _():
            body(turn)

    def sum_days(q):
        @pl.when(q >= DEEP)
        def _():
            for i in range(2):
                x_copies(0, q + i - DEEP).wait_send()

        both = counts[pl.ds(q, 2)].reshape(2 * half, chip_days)
        for s in range(2):

            @pl.when(q == 0)
            def _():
                share_days[s].wait()

            columns = slice(s * wide, s * wide + wide)
            whole = days[:, :, columns].reshape(chip_days, wide)
            total = jnp.dot(both, whole, preferred_element_type=jnp.float32).astype(part.dtype)
            for i in range(2):
                part[q + i, s] = total[i * half : i * half + half].reshape(part.shape[2:])
                scatter_one(q + i, s).start()

    def sum_pairs(q):
        x_copies(0, q).wait_recv()
        for s in range(2):
            kept = part[q, 1, :, v] if s else part[q, 0, u]
            pair[q, s] = kept + part_in[q, s]
        x_launch(1, scatter_two, q)

    def sum_chips(q):
        x_copies(1, q).wait_recv()
        for s in range(2):
            total = pair[q, s, second[s]].astype(jnp.float32) + pair_in[q, s].astype(jnp.float32)
            scaled = total * -vol[:, s * wide : s * wide + wide]
            shock[q + 1, c, u, v, :, s * wide : s * wide + wide] = scaled.astype(shock.dtype)
        x_launch(2, gather_one, q)

    def spread(q):
        x_copies(2, q).wait_recv()
        x_launch(3, gather_two, q)

    def cross(q):
        x_copies(3, q).wait_recv()

        @pl.when(q >= DEEP)
        def _():
            give_sibling(q - DEEP).wait_send()

        give_sibling(q).start()

    def revalue(r):
        @pl.when(r == 0)
        def _():
            load_book.wait()

        @pl.when(r > 0)
        def _():
            give_sibling(r - 1, False).wait_recv()

        moves = shock[r].reshape(2 * half, width)
        value = lax.dot_general(
            book[...], moves, (((1,), (1,)), ((), ())), preferred_element_type=jnp.float32
        ).astype(loss.dtype)
        few = mine // 2
        for h in range(2):
            for owner in range(16):
                at = (owner // 4, owner % 4) if h else (owner % 4, owner // 4)
                top = owner * mine + h * few
                loss[r, h, at[0], at[1]] = value[top : top + few]
        f_launch(0, pass_loss, r)

    def fold(r):
        f_copies(0, r).wait_recv()
        for h in range(2):
            total = loss[r, h, place[h][0]].astype(jnp.float32)
            for j in range(1, 4):
                total = total + loss_in[r, h, j - 1].astype(jnp.float32)
            row[r, h] = total.astype(row.dtype)
        f_launch(1, pass_row, r)

    def finish(r):
        few = mine // 2
        f_copies(1, r).wait_recv()
        for h in range(2):
            total = row[r, h, place[h][1]].astype(jnp.float32)
            for j in range(1, 4):
                total = total + row_in[r, h, j - 1].astype(jnp.float32)

            @pl.when(r > 0)
            def _():
                at = pl.multiple_of((r - 1) * 2 * half, 2 * half)
                out[h * few : h * few + few, pl.ds(at, 2 * half)] = total.astype(out.dtype)
                sums[h * few : h * few + few, :] = sums[h * few : h * few + few, :] + jnp.exp(total)

            @pl.when(r == 0)
            def _():
                owed[h * few : h * few + few, :] = total

    def turn(t, carry):
        stage(t - PAIRS, CHUNKS, sum_pairs)
        stage(t - CHIPS, CHUNKS, sum_chips)
        stage(t - SPREAD, CHUNKS, spread)
        stage(t - CROSS, CHUNKS, cross)
        stage(jnp.where(t % 2 == 0, t, -1), CHUNKS, sum_days)
        stage(t + 2, CHUNKS, count_days)
        stage(t - REVALUE, CHUNKS + 1, revalue)
        stage(t - FOLD, CHUNKS + 1, fold)
        stage(t - FINISH, CHUNKS + 1, finish)
        return carry

    lax.fori_loop(0, CHUNKS + 1 + FINISH, turn, 0)

    level = jnp.log(jnp.sum(sums[...], axis=1, keepdims=True) * (1.0 / paths))
    diagonal = lax.broadcasted_iota(jnp.int32, (mine, mine), 0) == lax.broadcasted_iota(
        jnp.int32, (mine, mine), 1
    )
    margin[...] = jnp.sum(jnp.where(diagonal, level, 0.0), axis=0, keepdims=True)
    over = owed[:, 0:1] - level
    shortfall[...] = jnp.sum(jnp.where(diagonal, over, 0.0), axis=0, keepdims=True)

    def sent(i, carry):
        for kind in range(2):
            f_copies(kind, CHUNKS - i).wait_send()
        for kind in range(4):
            x_copies(kind, CHUNKS - 1 - i).wait_send()
        give_sibling(CHUNKS - 1 - i).wait_send()
        return carry

    lax.fori_loop(0, DEEP, sent, 0)


def hand_over(*refs):
    for array, result in zip(refs[:3], refs[3:]):
        result[...] = array[...]


def local(history, block_starts, block_lengths, vol_scale, exposure, realized):
    own_days, width = history.shape
    paths = block_starts.shape[0]
    accounts = exposure.shape[0]
    mine = accounts // 16
    q, r = CHUNKS, CHUNKS + 1
    half = paths // q // 2
    block, wide, few = half // 4, width // 2, mine // 2
    vmem = pl.BlockSpec(memory_space=pltpu.VMEM)
    raw = pl.BlockSpec(memory_space=pl.ANY)
    bf16, f32 = jnp.bfloat16, jnp.float32
    dma = pltpu.SemaphoreType.DMA
    results = (
        jax.ShapeDtypeStruct((mine, paths), bf16),
        jax.ShapeDtypeStruct((1, mine), f32),
        jax.ShapeDtypeStruct((1, mine), f32),
    )
    found = pl.pallas_call(
        kernel,
        out_shape=results,
        in_specs=[raw, vmem, vmem, vmem, raw, vmem],
        out_specs=(vmem, vmem, vmem),
        scratch_shapes=[
            pltpu.VMEM((2, own_days, width), bf16),
            pltpu.VMEM((accounts, width), bf16),
            pltpu.VMEM((128, 128), f32),
            pltpu.VMEM((q, half, 2 * own_days), bf16),
            pltpu.VMEM((q, 2, 2, 2, block, wide), bf16),
            pltpu.VMEM((q, 2, 2, block, wide), bf16),
            pltpu.VMEM((q, 2, 2, block, wide), bf16),
            pltpu.VMEM((q, 2, block, wide), bf16),
            pltpu.VMEM((r, 2, 2, 2, block, width), bf16),
            pltpu.VMEM((r, 2, 4, 4, few, 2 * half), bf16),
            pltpu.VMEM((r, 2, 3, 4, few, 2 * half), bf16),
            pltpu.VMEM((r, 2, 4, few, 2 * half), bf16),
            pltpu.VMEM((r, 2, 3, few, 2 * half), bf16),
            pltpu.VMEM((mine, 2 * half), f32),
            pltpu.VMEM((mine, 2 * half), f32),
            dma((2,)),
            dma((2,)),
            dma((2,)),
            dma((4, DEEP)),
            dma((4, FAR)),
            dma((DEEP,)),
            dma((FAR,)),
            dma((2, DEEP)),
            dma((2, FAR)),
        ],
        compiler_params=pltpu.CompilerParams(
            collective_id=0, has_side_effects=True, vmem_limit_bytes=60 << 20
        ),
        name="backtest",
    )(history, block_starts.T, block_lengths.T, vol_scale.reshape(1, width), exposure, realized)
    out, margin, shortfall = pl.pallas_call(
        hand_over,
        out_shape=results,
        in_specs=[vmem] * 3,
        out_specs=(vmem,) * 3,
        name="results",
    )(*found)
    return out, margin.reshape(mine), shortfall.reshape(mine)


def solution(mesh):
    in_specs = (P("days", "fac"), P(), P(), P("fac"), P("days", "fac"), P("fac"))
    out_specs = (P(("days", "fac"), None), P(("days", "fac")), P(("days", "fac")))
    return jax.shard_map(local, mesh=mesh, in_specs=in_specs, out_specs=out_specs, check_vma=False)
```
